128 devices in a mesh: row: 16 (over y, x), col: 4 (over z), depth: 2 (over core).
Axes of the slice: x: 4, y: 4, z: 4, core: 2. Of those that a mesh axis runs over, the one named last changes fastest.
Arguments:
- tokens: bfloat16 [1024, 8192], P(('col', 'depth'), 'row'), may hold values from -6 to 6
- out_grad: bfloat16 [1024, 8192], P(('col', 'depth'), 'row'), may hold values from -6 to 6
- gate_weight: bfloat16 [8192, 14336], P('row', ('col', 'depth')), may hold values from -0.0625 to 0.0625
- up_weight: bfloat16 [8192, 14336], P('row', ('col', 'depth')), may hold values from -0.0625 to 0.0625
- down_weight: bfloat16 [8192, 14336], P('row', ('col', 'depth')), may hold values from -0.046875 to 0.046875
- gate_mask: int32 [128, 224], P('row', ('col', 'depth')), may hold values 0 or 1
- up_mask: int32 [128, 224], P('row', ('col', 'depth')), may hold values 0 or 1
- down_mask: int32 [128, 224], P('row', ('col', 'depth')), may hold values 0 or 1
Outputs:
- output: float32 [1024, 8192], P(('col', 'depth'), 'row')
- in_grad: float32 [1024, 8192], P(('col', 'depth'), 'row')
- gate_grad: float32 [8192, 14336], P('row', ('col', 'depth'))
- up_grad: float32 [8192, 14336], P('row', ('col', 'depth'))
- down_grad: float32 [8192, 14336], P('row', ('col', 'depth'))
The draws below stay inside these ranges and needn't reach their ends.
All inputs are finite; a program needn't handle non-finite values. No bound on the sum of `gate_mask` or of `up_mask` or of `down_mask` on one device may be relied on, other than what follows from the above.
Results may differ from the reference program's by a relative error of at most 0.0029.
Values may be sent and summed in bfloat16 or wider, within the bound.
No kernel may reach another device: no remote copies, remote signals or barrier semaphores. Data moves between devices by JAX's collectives and lax.ppermute only.
A program may use at most 192 MiB of HBM per device.

```python
import jax
import jax.numpy as jnp

D = 8192
FF = 14336
BLOCK = 64
TOKENS = 1024


def plant(drawn, stream_key, low, largest):
    index_at = [jax.random.randint(jax.random.fold_in(stream_key, axis), (), 0, length) for axis, length in enumerate(drawn.shape)]
    widest = drawn.shape.index(max(drawn.shape))
    beside = index_at[:widest] + [(index_at[widest] + 1) % drawn.shape[widest]] + index_at[widest + 1:]
    return drawn.at[tuple(index_at)].set(low).at[tuple(beside)].set(largest)


def block_levels(key, dims, split, least, high):
    def one(axis_at, blocks):
        heights = jax.random.uniform(jax.random.fold_in(jax.random.fold_in(key, 6), axis_at), (blocks,), jnp.float32, least / len(split), high / len(split))
        return jnp.repeat(jnp.exp(heights), dims[axis_at] // blocks).reshape((-1,) + (1,) * (len(dims) - axis_at - 1))

    loudness = one(*split[0])
    for cut in split[1:]:
        loudness = loudness * one(*cut)
    return loudness


def bell_draw(key, dims, width, reach, pieces=(), dtype=jnp.bfloat16):
    values = width * jax.random.normal(key, dims, jnp.float32)
    if pieces:
        values = values * block_levels(key, dims, pieces, -0.22, 0.18)
    return jnp.clip(values, -reach, reach).astype(dtype)


def setup_inputs(seed: int = 0) -> dict:
    streams_of = jax.random.split(jax.random.key(seed), 9)
    tokens = bell_draw(streams_of[0], (TOKENS, D), 1.0, 6.0, ((0, 8), (1, 16)))
    out_grad = bell_draw(streams_of[1], (TOKENS, D), 1.0, 6.0, ((0, 8), (1, 16)))
    gate_weight = bell_draw(streams_of[2], (D, FF), D ** -0.5, 0.0625, ((0, 16), (1, 8)))
    up_weight = bell_draw(streams_of[3], (D, FF), D ** -0.5, 0.0625, ((0, 16), (1, 8)))
    down_weight = bell_draw(streams_of[4], (D, FF), FF ** -0.5, 0.046875, ((0, 16), (1, 8)))
    gate_mask = plant((jax.random.randint(streams_of[5], (D // BLOCK, FF // BLOCK), 0, 2) < 1).astype(jnp.int32), jax.random.fold_in(streams_of[5], 1), 0, 1)
    up_mask = plant((jax.random.randint(streams_of[6], (D // BLOCK, FF // BLOCK), 0, 2) < 1).astype(jnp.int32), jax.random.fold_in(streams_of[6], 1), 0, 1)
    down_mask = plant((jax.random.randint(streams_of[7], (D // BLOCK, FF // BLOCK), 0, 2) < 1).astype(jnp.int32), jax.random.fold_in(streams_of[7], 1), 0, 1)
    return dict(tokens=tokens, out_grad=out_grad, gate_weight=gate_weight, up_weight=up_weight, down_weight=down_weight, gate_mask=gate_mask, up_mask=up_mask, down_mask=down_mask)


def expand(mask):
    return jnp.repeat(jnp.repeat(mask, BLOCK, axis=0), BLOCK, axis=1)


def reference(tokens, out_grad, gate_weight, up_weight, down_weight, gate_mask, up_mask, down_mask):
    mask_gate = expand(gate_mask)
    mask_up = expand(up_mask)
    mask_down = expand(down_mask)
    masked_gate = gate_weight * mask_gate.astype(jnp.bfloat16)
    masked_up = up_weight * mask_up.astype(jnp.bfloat16)
    masked_down = down_weight * mask_down.astype(jnp.bfloat16)
    gate = jnp.dot(tokens, masked_gate, preferred_element_type=jnp.float32)
    up = jnp.dot(tokens, masked_up, preferred_element_type=jnp.float32)
    sig = jax.nn.sigmoid(gate)
    act = gate * sig
    hidden = (act * up).astype(jnp.bfloat16)
    output = jnp.dot(hidden, masked_down.T, preferred_element_type=jnp.float32)
    hidden_grad = jnp.dot(out_grad, masked_down, preferred_element_type=jnp.float32)
    gate_term = (hidden_grad * up * sig * (1.0 + gate * (1.0 - sig))).astype(jnp.bfloat16)
    up_term = (hidden_grad * act).astype(jnp.bfloat16)
    in_grad = jnp.dot(gate_term, masked_gate.T, preferred_element_type=jnp.float32) + jnp.dot(up_term, masked_up.T, preferred_element_type=jnp.float32)
    gate_grad = jnp.dot(tokens.T, gate_term, preferred_element_type=jnp.float32) * mask_gate.astype(jnp.float32)
    up_grad = jnp.dot(tokens.T, up_term, preferred_element_type=jnp.float32) * mask_up.astype(jnp.float32)
    down_grad = jnp.dot(out_grad.T, hidden, preferred_element_type=jnp.float32) * mask_down.astype(jnp.float32)
    return (output, in_grad, gate_grad, up_grad, down_grad)
```

```python
import functools

import jax
import jax.numpy as jnp
from jax import lax
from jax.experimental import pallas as pl
from jax.experimental.pallas import tpu as pltpu
from jax.sharding import PartitionSpec as P


BF16 = jnp.bfloat16
F16 = jnp.float16
F32 = jnp.float32
SIDE = 4
SCALE = 16.0
MIB = 1 << 20


def send(values, axis, shift):
    if axis == "x":
        perm = [(y * SIDE + x, y * SIDE + (x + shift) % SIDE) for y in range(SIDE) for x in range(SIDE)]
        return lax.ppermute(values, "row", perm)
    if axis == "y":
        perm = [(y * SIDE + x, (y + shift) % SIDE * SIDE + x) for y in range(SIDE) for x in range(SIDE)]
        return lax.ppermute(values, "row", perm)
    if axis == "z":
        return lax.ppermute(values, "col", [(z, (z + shift) % SIDE) for z in range(SIDE)])
    return lax.ppermute(values, "depth", [(0, 1), (1, 0)])


def row_mask(mask, width, first, block):
    rows = lax.broadcasted_iota(jnp.int32, (mask.shape[1], width), 0)
    cols = lax.broadcasted_iota(jnp.int32, (mask.shape[1], width), 1) + first
    spread = jnp.logical_and(cols >= rows * block, cols < (rows + 1) * block).astype(F32)
    return jnp.dot(mask.astype(F32), spread, preferred_element_type=F32)


def mask_kernel(block, gate_mask, up_mask, down_mask, gate, up, down, gate_out, up_out, down_out):
    width = gate.shape[1]
    for mask, weight, out in ((gate_mask, gate, gate_out), (up_mask, up, up_out), (down_mask, down, down_out)):
        wide = row_mask(jnp.broadcast_to(mask[0], (8, mask.shape[2])), width, 0, block)
        out[...] = (weight[...].astype(F32) * wide[0:1]).astype(BF16)


def mask_weights(weights, masks):
    rows, width = weights[0].shape
    mrows, mcols = masks[0].shape
    block = rows // mrows
    mask_spec = pl.BlockSpec((1, 1, mcols), lambda i: (i, 0, 0))
    spec = pl.BlockSpec((block, width), lambda i: (i, 0))
    return pl.pallas_call(
        functools.partial(mask_kernel, block),
        grid=(mrows,),
        in_specs=[mask_spec] * 3 + [spec] * 3,
        out_specs=[spec] * 3,
        out_shape=[jax.ShapeDtypeStruct((rows, width), BF16)] * 3,
        name="mask_weights",
    )(*[m.reshape(mrows, 1, mcols) for m in masks], *weights)


def source_row(place, near, far, x_first):
    step_x, step_y = (near, far) if x_first else (far, near)
    return lax.rem(place[0] + step_y, SIDE) * 128 + lax.rem(place[1] + step_x, SIDE) * 32


def roll_kernel(x_first, rows_each, place, tokens, *outs):
    for near in range(SIDE):
        for far in range(SIDE):
            start = pl.multiple_of(source_row(place, near, far, x_first), 32)
            at = (near * SIDE + far) * 32
            outs[at // rows_each][pl.ds(at % rows_each, 32), :] = tokens[pl.ds(start, 32), :]


def roll_tokens(tokens, place, x_first, rows_each):
    count = tokens.shape[0] // rows_each
    return pl.pallas_call(
        functools.partial(roll_kernel, x_first, rows_each),
        in_specs=[pl.BlockSpec(memory_space=pltpu.SMEM), pl.BlockSpec(memory_space=pltpu.VMEM)],
        out_specs=[pl.BlockSpec(memory_space=pltpu.VMEM)] * count,
        out_shape=[jax.ShapeDtypeStruct((rows_each, tokens.shape[1]), BF16)] * count,
        name="roll_tokens",
    )(place, tokens)


def fill(scratch, refs):
    at = 0
    for ref in refs:
        scratch[pl.ds(at, ref.shape[0]), :] = ref[...]
        at += ref.shape[0]


def unroll_store(place, acc, keep, give):
    for out, x_first, base in ((keep, True, 0), (give, False, 512)):
        for near in range(SIDE):
            for far in range(SIDE):
                start = pl.multiple_of(source_row(place, near, far, x_first), 32)
                out[pl.ds(start, 32), :] = acc[pl.ds(base + (near * SIDE + far) * 32, 32), :]


def masked_store(out, grad, mask, first, block):
    wide = row_mask(mask, out.shape[1], first, block)
    for i in range(mask.shape[0]):
        at = pl.ds(i * block, block)
        out[at, :] = grad[i * block:(i + 1) * block] * wide[i:i + 1]


def grads_kernel(counts, block, *refs):
    n_tok, *n_terms = counts
    take = iter(refs)
    tokens = [next(take) for _ in range(n_tok)]
    terms = [[next(take) for _ in range(n)] for n in n_terms]
    masks = [next(take) for _ in n_terms]
    outs = [next(take) for _ in n_terms]
    flipped, joined = take
    step = pl.program_id(0)

    @pl.when(step == 0)
    def _():
        at = 0
        for ref in tokens:
            flipped[:, pl.ds(at, ref.shape[0])] = ref[...].T
            at += ref.shape[0]

    for pieces, mask, out in zip(terms, masks, outs):
        fill(joined, pieces)
        grad = jnp.dot(flipped[...], joined[...], preferred_element_type=F32)
        masked_store(out, grad, mask[...], step * out.shape[1], block)


def weight_grads(tokens, terms, masks, wide=256):
    features = tokens[0].shape[1]
    width = terms[0][0].shape[1]
    total = sum(t.shape[0] for t in tokens)
    counts = (len(tokens),) + tuple(len(t) for t in terms)
    whole = pl.BlockSpec(memory_space=pltpu.VMEM)
    block = features // masks[0].shape[0]
    return pl.pallas_call(
        functools.partial(grads_kernel, counts, block),
        grid=(width // wide,),
        in_specs=[whole] * len(tokens)
        + [pl.BlockSpec((piece.shape[0], wide), lambda f: (0, f)) for pieces in terms for piece in pieces]
        + [whole] * len(terms),
        out_specs=[pl.BlockSpec((features, wide), lambda f: (0, f))] * len(terms),
        out_shape=[jax.ShapeDtypeStruct((features, width), F32)] * len(terms),
        scratch_shapes=[pltpu.VMEM((features, total), BF16), pltpu.VMEM((total, wide), BF16)],
        compiler_params=pltpu.CompilerParams(vmem_limit_bytes=24 * MIB),
        name="weight_grads",
    )(*tokens, *[piece for pieces in terms for piece in pieces], *masks)


def back_kernel(counts, steps, place, *refs):
    take = iter(refs)
    terms = [[next(take) for _ in range(n)] for n in counts]
    weights = [next(take) for _ in counts]
    keep, give, acc, joined = take
    step = pl.program_id(0)
    total = None
    for pieces, weight in zip(terms, weights):
        fill(joined, pieces)
        part = lax.dot_general(
            joined[...], weight[...], (((1,), (1,)), ((), ())), preferred_element_type=F32
        )
        total = part if total is None else total + part

    @pl.when(step == 0)
    def _():
        acc[...] = total

    @pl.when(step > 0)
    def _():
        acc[...] += total

    @pl.when(step == steps - 1)
    def _():
        unroll_store(place, acc, keep, give)


def back_product(terms, weights, place, wide=256):
    features, width = weights[0].shape
    total = sum(t.shape[0] for t in terms[0])
    counts = tuple(len(t) for t in terms)
    steps = width // wide
    whole = pl.BlockSpec((total // 2, features), lambda f: (0, 0))
    return pl.pallas_call(
        functools.partial(back_kernel, counts, steps),
        grid=(steps,),
        in_specs=[pl.BlockSpec(memory_space=pltpu.SMEM)]
        + [pl.BlockSpec((piece.shape[0], wide), lambda f: (0, f)) for pieces in terms for piece in pieces]
        + [pl.BlockSpec((features, wide), lambda f: (0, f))] * len(weights),
        out_specs=[whole] * 2,
        out_shape=[jax.ShapeDtypeStruct((total // 2, features), F32)] * 2,
        scratch_shapes=[pltpu.VMEM((total, features), F32), pltpu.VMEM((total, wide), BF16)],
        compiler_params=pltpu.CompilerParams(vmem_limit_bytes=24 * MIB),
        name="back_product",
    )(place, *[piece for pieces in terms for piece in pieces], *weights)


def gather_tokens(own):
    mine = jnp.concatenate([own] + [send(own, "z", -shift) for shift in (1, 2, 3)], axis=0)
    return mine, send(mine, "core", 1)


def partial(tokens, weight):
    return jnp.dot(tokens, weight, preferred_element_type=F32) * SCALE


def sum_first(units, axis):
    halfway = [send(partial(pieces[2], w).astype(F16), axis, way) for pieces, w, way in units]
    away = [send(partial(pieces[-way], w).astype(F16), axis, -way) for pieces, w, way in units]
    there = [
        send((partial(pieces[way], w) + met.astype(F32)).astype(F16), axis, way)
        for (pieces, w, way), met in zip(units, halfway)
    ]
    return [
        (partial(pieces[0], w) + a.astype(F32) + t.astype(F32)).astype(F16)
        for (pieces, w, _), a, t in zip(units, away, there)
    ]


def sum_second(blocks, axis):
    got = [send(blocks[shift], axis, shift) for shift in (1, 2, 3)]
    total = blocks[0].astype(F32)
    for values in got:
        total = total + values.astype(F32)
    return total * (1.0 / SCALE)


def collect(values, axis):
    return [values] + [send(values, axis, -shift) for shift in (1, 2, 3)]


def per_device(
    tokens, out_grad, gate_weight, up_weight, down_weight, gate_mask, up_mask, down_mask
):
    row = lax.axis_index("row")
    place = jnp.stack([row // SIDE, row % SIDE]).astype(jnp.int32)
    w_gate, w_up, w_down = mask_weights((gate_weight, up_weight, down_weight), (gate_mask, up_mask, down_mask))
    halves = (("x", "y", True), ("y", "x", False))

    groups = gather_tokens(tokens)
    ins = [roll_tokens(g, place, h[2], 128) for g, h in zip(groups, halves)]
    groups = gather_tokens(out_grad)
    outs = [roll_tokens(g, place, h[2], 64) for g, h in zip(groups, halves)]

    near = []
    for (first, _, _), pieces in zip(halves, ins):
        near.append(sum_first([(pieces, w_gate, 1), (pieces, w_up, -1)], first))
    gate_up = []
    for (_, second, _), (g, u) in zip(halves, near):
        blocks = [jnp.stack([g[i * 32:(i + 1) * 32], u[i * 32:(i + 1) * 32]]) for i in range(SIDE)]
        gate_up.append(sum_second(blocks, second))
    acts = [(gate * jax.nn.sigmoid(gate), up) for gate, up in gate_up]

    near = []
    for (first, _, _), pieces in zip(halves, outs):
        near.append(sum_first([(pieces[0::2], w_down, 1), (pieces[1::2], w_down, -1)], first))
    hidden_grads = []
    for (_, second, _), (low, high) in zip(halves, near):
        hidden_grads.append(sum_second([low[:32], low[32:], high[:32], high[32:]], second))

    hidden = []
    for (first, second, _), (act, up) in zip(halves, acts):
        mine = jnp.concatenate(collect((act * up).astype(BF16), second), axis=0)
        left, right = send(mine, first, 1), send(mine, first, -1)
        far = [send(left[:64], first, 1), send(right[64:], first, -1)]
        hidden += [mine, right, *far, left]

    out_keep, out_give = back_product([hidden], [w_down], place)
    (down_grad,) = weight_grads(outs[0] + outs[1], [hidden], [down_mask])

    gate_terms, up_terms = [], []
    for (first, second, _), (gate, up), (act, _), grad in zip(halves, gate_up, acts, hidden_grads):
        sig = jax.nn.sigmoid(gate)
        gate_term = (grad * up * sig * (1.0 + gate * (1.0 - sig))).astype(BF16)
        up_term = (grad * act).astype(BF16)
        both = collect(jnp.stack([gate_term, up_term]), second)
        for at, way, terms in ((0, 1, gate_terms), (1, -1, up_terms)):
            mine = jnp.concatenate([b[at] for b in both], axis=0)
            left, right = send(mine, first, 1), send(mine, first, -1)
            far = send(left if way == 1 else right, first, way)
            terms += [mine, right, far, left]

    in_keep, in_give = back_product([gate_terms, up_terms], [w_gate, w_up], place)
    gate_grad, up_grad = weight_grads(ins[0] + ins[1], [gate_terms, up_terms], [gate_mask, up_mask])

    results = []
    for keep, give in ((out_keep, out_give), (in_keep, in_give)):
        chip = (keep + send(give, "core", 1)).reshape(SIDE, 128, keep.shape[1])
        total = chip[0]
        for shift in (1, 2, 3):
            total = total + send(chip[shift].astype(BF16), "z", shift).astype(F32)
        results.append(total)
    return (results[0], results[1], gate_grad, up_grad, down_grad)


def solution(mesh):
    data, weight = P(("col", "depth"), "row"), P("row", ("col", "depth"))
    return jax.shard_map(
        per_device,
        mesh=mesh,
        in_specs=(data,) * 2 + (weight,) * 6,
        out_specs=(data,) * 2 + (weight,) * 3,
        check_vma=False,
    )
```

```python
import functools

import jax
import jax.numpy as jnp
from jax import lax
from jax.experimental import pallas as pl
from jax.experimental.pallas import tpu as pltpu
from jax.sharding import PartitionSpec as P


BF16 = jnp.bfloat16
F16 = jnp.float16
F32 = jnp.float32
SIDE = 4
SCALE = 16.0
MIB = 1 << 20


def send(values, axis, shift):
    if axis == "core":
        return lax.ppermute(values, "depth", [(0, 1), (1, 0)])
    if axis == "z":
        return lax.ppermute(values, "col", [(z, (z + shift) % SIDE) for z in range(SIDE)])
    perm = []
    for y in range(SIDE):
        for x in range(SIDE):
            for core in range(2):
                along_x = (core == 0) == (axis == "first")
                to_y, to_x = (y, (x + shift) % SIDE) if along_x else ((y + shift) % SIDE, x)
                perm.append(((y * SIDE + x) * 2 + core, (to_y * SIDE + to_x) * 2 + core))
    return lax.ppermute(values, ("row", "depth"), perm)


def row_mask(mask, width, first, block):
    rows = lax.broadcasted_iota(jnp.int32, (mask.shape[1], width), 0)
    cols = lax.broadcasted_iota(jnp.int32, (mask.shape[1], width), 1) + first
    spread = jnp.logical_and(cols >= rows * block, cols < (rows + 1) * block).astype(F32)
    return jnp.dot(mask.astype(F32), spread, preferred_element_type=F32)


def mask_kernel(block, gate_mask, up_mask, down_mask, gate, up, down, gate_up_out, down_out):
    width = gate.shape[1]
    for mask, weight, out, first in (
        (gate_mask, gate, gate_up_out, 0), (up_mask, up, gate_up_out, width), (down_mask, down, down_out, 0)
    ):
        wide = row_mask(jnp.broadcast_to(mask[0], (8, mask.shape[2])), width, 0, block)
        out[:, pl.ds(first, width)] = (weight[...].astype(F32) * wide[0:1]).astype(BF16)


def mask_weights(weights, masks):
    rows, width = weights[0].shape
    mrows, mcols = masks[0].shape
    block = rows // mrows
    mask_spec = pl.BlockSpec((1, 1, mcols), lambda i: (i, 0, 0))
    spec = pl.BlockSpec((block, width), lambda i: (i, 0))
    return pl.pallas_call(
        functools.partial(mask_kernel, block),
        grid=(mrows,),
        in_specs=[mask_spec] * 3 + [spec] * 3,
        out_specs=[pl.BlockSpec((block, 2 * width), lambda i: (i, 0)), spec],
        out_shape=[jax.ShapeDtypeStruct((rows, 2 * width), BF16), jax.ShapeDtypeStruct((rows, width), BF16)],
        name="mask_weights",
    )(*[m.reshape(mrows, 1, mcols) for m in masks], *weights)


def join_kernel(*refs):
    out = refs[-1]
    at = 0
    for ref in refs[:-1]:
        out[pl.ds(at, ref.shape[0]), :] = ref[...]
        at += ref.shape[0]


def join_rows(pieces):
    rows = sum(p.shape[0] for p in pieces)
    return pl.pallas_call(
        join_kernel,
        in_specs=[pl.BlockSpec(memory_space=pltpu.VMEM)] * len(pieces),
        out_specs=pl.BlockSpec(memory_space=pltpu.VMEM),
        out_shape=jax.ShapeDtypeStruct((rows, pieces[0].shape[1]), pieces[0].dtype),
        name="join_rows",
    )(*pieces)


def block_row(place, near, far):
    return lax.rem(place[0] + near, SIDE), lax.rem(place[1] + far, SIDE) * 64


PIECES = (
    ((2, 0), (2, 1), (1, 2), (1, 3)),
    ((2, 2), (2, 3), (3, 0), (3, 1)),
    ((1, 0), (1, 1)),
    ((3, 2), (3, 3)),
    ((0, 0), (0, 1)),
    ((0, 2), (0, 3)),
)


def roll_kernel(place, mine, theirs, *outs):
    for out, blocks in zip(outs, PIECES):
        for i, (near, far) in enumerate(blocks):
            big, small = block_row(place, near, far)
            to = pl.ds(i * 64, 64)

            @pl.when(big < 2)
            def _():
                out[to, :] = mine[pl.ds(pl.multiple_of(big * 256 + small, 64), 64), :]

            @pl.when(big >= 2)
            def _():
                out[to, :] = theirs[pl.ds(pl.multiple_of((big - 2) * 256 + small, 64), 64), :]


def roll_tokens(mine, theirs, place):
    features = mine.shape[1]
    return pl.pallas_call(
        roll_kernel,
        in_specs=[pl.BlockSpec(memory_space=pltpu.SMEM)] + [pl.BlockSpec(memory_space=pltpu.VMEM)] * 2,
        out_specs=[pl.BlockSpec(memory_space=pltpu.VMEM)] * len(PIECES),
        out_shape=[jax.ShapeDtypeStruct((64 * len(p), features), BF16) for p in PIECES],
        name="roll_tokens",
    )(place, mine, theirs)


def fill(scratch, refs):
    at = 0
    for ref in refs:
        scratch[pl.ds(at, ref.shape[0]), :] = ref[...]
        at += ref.shape[0]


def masked_store(out, grad, mask, first, block):
    wide = row_mask(mask, out.shape[1], first, block)
    for i in range(mask.shape[0]):
        at = pl.ds(i * block, block)
        out[at, :] = grad[i * block:(i + 1) * block] * wide[i:i + 1]


def grads_kernel(n_pieces, n_terms, block, *refs):
    take = iter(refs)
    tokens = [next(take) for _ in PIECES]
    terms = [[next(take) for _ in range(n_pieces)] for _ in range(n_terms)]
    masks = [next(take) for _ in range(n_terms)]
    outs = [next(take) for _ in range(n_terms)]
    flipped, joined = take
    step = pl.program_id(0)

    @pl.when(step == 0)
    def _():
        for ref, blocks in zip(tokens, PIECES):
            for i in range(0, len(blocks), 2):
                near, far = blocks[i]
                flipped[:, pl.ds((near * SIDE + far) * 64, 128)] = ref[pl.ds(i * 64, 128), :].T

    for pieces, mask, out in zip(terms, masks, outs):
        fill(joined, pieces)
        grad = jnp.dot(flipped[...], joined[...], preferred_element_type=F32)
        masked_store(out, grad, mask[...], step * out.shape[1], block)


def term_specs(pieces, n_terms, steps, wide):
    return [
        pl.BlockSpec((piece.shape[0], wide), functools.partial(lambda at, f: (0, at + f), term * steps))
        for term in range(n_terms)
        for piece in pieces
    ]


def weight_grads(tokens, pieces, masks, wide=256):
    features = tokens[0].shape[1]
    n_terms = len(masks)
    width = pieces[0].shape[1] // n_terms
    total = sum(p.shape[0] for p in pieces)
    whole = pl.BlockSpec(memory_space=pltpu.VMEM)
    block = features // masks[0].shape[0]
    return pl.pallas_call(
        functools.partial(grads_kernel, len(pieces), n_terms, block),
        grid=(width // wide,),
        in_specs=[whole] * len(tokens) + term_specs(pieces, n_terms, width // wide, wide) + [whole] * n_terms,
        out_specs=[pl.BlockSpec((features, wide), lambda f: (0, f))] * n_terms,
        out_shape=[jax.ShapeDtypeStruct((features, width), F32)] * n_terms,
        scratch_shapes=[pltpu.VMEM((features, total), BF16), pltpu.VMEM((total, wide), BF16)],
        compiler_params=pltpu.CompilerParams(vmem_limit_bytes=24 * MIB),
        name="weight_grads",
    )(*tokens, *(list(pieces) * n_terms), *masks)


def back_kernel(n_pieces, n_terms, steps, place, *refs):
    take = iter(refs)
    terms = [[next(take) for _ in range(n_pieces)] for _ in range(n_terms)]
    weights = [next(take) for _ in range(n_terms)]
    keep, give, acc, joined = take
    step = pl.program_id(0)
    total = None
    for pieces, weight in zip(terms, weights):
        fill(joined, pieces)
        part = lax.dot_general(
            joined[...], weight[...], (((1,), (1,)), ((), ())), preferred_element_type=F32
        )
        total = part if total is None else total + part

    @pl.when(step == 0)
    def _():
        acc[...] = total

    @pl.when(step > 0)
    def _():
        acc[...] += total

    @pl.when(step == steps - 1)
    def _():
        for near in range(SIDE):
            for far in range(SIDE):
                big, small = block_row(place, near, far)
                at = pl.ds((near * SIDE + far) * 64, 64)

                @pl.when(big < 2)
                def _():
                    keep[pl.ds(pl.multiple_of(big * 256 + small, 64), 64), :] = acc[at, :]

                @pl.when(big >= 2)
                def _():
                    give[pl.ds(pl.multiple_of((big - 2) * 256 + small, 64), 64), :] = acc[at, :]


def back_product(pieces, weights, n_terms, place, wide=256):
    features = weights.shape[0]
    width = weights.shape[1] // n_terms
    total = sum(p.shape[0] for p in pieces)
    steps = width // wide
    half = pl.BlockSpec((total // 2, features), lambda f: (0, 0))
    return pl.pallas_call(
        functools.partial(back_kernel, len(pieces), n_terms, steps),
        grid=(steps,),
        in_specs=[pl.BlockSpec(memory_space=pltpu.SMEM)]
        + term_specs(pieces, n_terms, steps, wide)
        + term_specs([weights], n_terms, steps, wide),
        out_specs=[half] * 2,
        out_shape=[jax.ShapeDtypeStruct((total // 2, features), F32)] * 2,
        scratch_shapes=[pltpu.VMEM((total, features), F32), pltpu.VMEM((total, wide), BF16)],
        compiler_params=pltpu.CompilerParams(vmem_limit_bytes=24 * MIB),
        name="back_product",
    )(place, *(list(pieces) * n_terms), *([weights] * n_terms))


def partial(tokens, weight):
    return jnp.dot(tokens, weight, preferred_element_type=F32) * SCALE


def sum_first(pieces, weight):
    both_up, both_down, up, down, low, high = pieces
    from_left = send(partial(both_up, weight).astype(F16), "first", 1)
    from_right = send(partial(both_down, weight).astype(F16), "first", -1)
    low_left = send((partial(up, weight) + from_left[:128].astype(F32)).astype(F16), "first", 1)
    high_right = send((partial(down, weight) + from_right[:128].astype(F32)).astype(F16), "first", -1)
    low_sum = partial(low, weight) + from_right[128:].astype(F32) + low_left.astype(F32)
    high_sum = partial(high, weight) + from_left[128:].astype(F32) + high_right.astype(F32)
    return low_sum.astype(F16), high_sum.astype(F16)


def sum_second(low, high):
    total = low[:64].astype(F32)
    for shift, values in ((1, low[64:]), (3, high[64:]), (2, high[:64])):
        total = total + send(values, "second", shift).astype(F32)
    return total * (1.0 / SCALE)


def gather_plane(values):
    mine = jnp.concatenate([values] + [send(values, "second", -shift) for shift in (1, 2, 3)], axis=0)
    left, right = send(mine, "first", 1), send(mine, "first", -1)
    return [mine, right, send(left[:128], "first", 1), send(right[128:], "first", -1), left]


def gather_tokens(own):
    mine = join_rows([own] + [send(own, "z", -shift) for shift in (1, 2, 3)])
    return mine, send(mine, "core", 1)


def sum_tokens(keep, give):
    chip = (keep + send(give, "core", 1)).reshape(SIDE, 128, keep.shape[1])
    total = chip[0]
    for shift in (1, 2, 3):
        total = total + send(chip[shift].astype(BF16), "z", shift).astype(F32)
    return total


def per_device(
    tokens, out_grad, gate_weight, up_weight, down_weight, gate_mask, up_mask, down_mask
):
    row, core = lax.axis_index("row"), lax.axis_index("depth")
    y, x = row // SIDE, row % SIDE
    place = jnp.where(core == 0, jnp.stack([x, y]), jnp.stack([y, x])).astype(jnp.int32)
    w_gate_up, w_down = mask_weights((gate_weight, up_weight, down_weight), (gate_mask, up_mask, down_mask))
    width = w_down.shape[1]

    ins = roll_tokens(*gather_tokens(tokens), place)
    outs = roll_tokens(*gather_tokens(out_grad), place)
    near_gate_up = sum_first(ins, w_gate_up)
    near_grad = sum_first(outs, w_down)

    gate_up = sum_second(*near_gate_up)
    gate, up = gate_up[:, :width], gate_up[:, width:]
    sig = jax.nn.sigmoid(gate)
    act = gate * sig
    hidden = gather_plane((act * up).astype(BF16))

    grad = sum_second(*near_grad)
    gate_term = (grad * up * sig * (1.0 + gate * (1.0 - sig))).astype(BF16)
    up_term = (grad * act).astype(BF16)
    terms = gather_plane(jnp.concatenate([gate_term, up_term], axis=1))

    output = sum_tokens(*back_product(hidden, w_down, 1, place))
    (down_grad,) = weight_grads(outs, hidden, [down_mask])
    in_grad = sum_tokens(*back_product(terms, w_gate_up, 2, place))
    gate_grad, up_grad = weight_grads(ins, terms, [gate_mask, up_mask])
    return (output, in_grad, gate_grad, up_grad, down_grad)


def solution(mesh):
    data, weight = P(("col", "depth"), "row"), P("row", ("col", "depth"))
    return jax.shard_map(
        per_device,
        mesh=mesh,
        in_specs=(data,) * 2 + (weight,) * 6,
        out_specs=(data,) * 2 + (weight,) * 3,
        check_vma=False,
    )
```

```python
import functools

import jax
import jax.numpy as jnp
from jax import lax
from jax.experimental import pallas as pl
from jax.experimental.pallas import tpu as pltpu
from jax.sharding import PartitionSpec as P


BF16 = jnp.bfloat16
F16 = jnp.float16
F32 = jnp.float32
SIDE = 4
SCALE = 16.0
MIB = 1 << 20


def send(values, axis, shift):
    if axis == "core":
        return lax.ppermute(values, "depth", [(0, 1), (1, 0)])
    if axis == "z":
        return lax.ppermute(values, "col", [(z, (z + shift) % SIDE) for z in range(SIDE)])
    perm = []
    for y in range(SIDE):
        for x in range(SIDE):
            for core in range(2):
                along_x = (core == 0) == (axis == "first")
                to_y, to_x = (y, (x + shift) % SIDE) if along_x else ((y + shift) % SIDE, x)
                perm.append(((y * SIDE + x) * 2 + core, (to_y * SIDE + to_x) * 2 + core))
    return lax.ppermute(values, ("row", "depth"), perm)


def row_mask(mask, width, first, block):
    rows = lax.broadcasted_iota(jnp.int32, (mask.shape[1], width), 0)
    cols = lax.broadcasted_iota(jnp.int32, (mask.shape[1], width), 1) + first
    spread = jnp.logical_and(cols >= rows * block, cols < (rows + 1) * block).astype(F32)
    return jnp.dot(mask.astype(F32), spread, preferred_element_type=F32)


def mask_kernel(block, gate_mask, up_mask, down_mask, gate, up, down, gate_up_out, down_out):
    width = gate.shape[1]
    for mask, weight, out, first in (
        (gate_mask, gate, gate_up_out, 0), (up_mask, up, gate_up_out, width), (down_mask, down, down_out, 0)
    ):
        wide = row_mask(jnp.broadcast_to(mask[0], (8, mask.shape[2])), width, 0, block)
        out[:, pl.ds(first, width)] = (weight[...].astype(F32) * wide[0:1]).astype(BF16)


def mask_weights(weights, masks):
    rows, width = weights[0].shape
    mrows, mcols = masks[0].shape
    block = rows // mrows
    mask_spec = pl.BlockSpec((1, 1, mcols), lambda i: (i, 0, 0))
    spec = pl.BlockSpec((block, width), lambda i: (i, 0))
    return pl.pallas_call(
        functools.partial(mask_kernel, block),
        grid=(mrows,),
        in_specs=[mask_spec] * 3 + [spec] * 3,
        out_specs=[pl.BlockSpec((block, 2 * width), lambda i: (i, 0)), spec],
        out_shape=[jax.ShapeDtypeStruct((rows, 2 * width), BF16), jax.ShapeDtypeStruct((rows, width), BF16)],
        compiler_params=pltpu.CompilerParams(vmem_limit_bytes=8 * MIB),
        name="mask_weights",
    )(*[m.reshape(mrows, 1, mcols) for m in masks], *weights)


ORDER = ((2, 0), (1, 1), (2, 1), (3, 0), (1, 0), (3, 1), (0, 0), (0, 1))


def my_place():
    row, core = lax.axis_index("row"), lax.axis_index("depth")
    y, x = row // SIDE, lax.rem(row, SIDE)
    return jnp.where(core == 0, x, y), jnp.where(core == 0, y, x)


def roll_kernel(order, *refs):
    *pieces, out, sems = refs
    first, second = my_place()
    copies = []
    for i in range(16):
        near = lax.rem(i // SIDE + SIDE - first, SIDE)
        far = lax.rem(i % SIDE + SIDE - second, SIDE)
        to = pl.multiple_of(order[near * 2 + far // 2] * 128 + lax.rem(far, 2) * 64, 64)
        copy = pltpu.make_async_copy(
            pieces[i // 2].at[pl.ds(i % 2 * 64, 64), :], out.at[pl.ds(to, 64), :], sems.at[i]
        )
        copy.start()
        copies.append(copy)
    for copy in copies:
        copy.wait()


def roll_tokens(pieces):
    order = jnp.array([ORDER.index((i // 2, i % 2)) for i in range(8)], jnp.int32)
    return pl.pallas_call(
        roll_kernel,
        in_specs=[pl.BlockSpec(memory_space=pltpu.SMEM)] + [pl.BlockSpec(memory_space=pl.ANY)] * len(pieces),
        out_specs=pl.BlockSpec(memory_space=pl.ANY),
        out_shape=jax.ShapeDtypeStruct((128 * len(pieces), pieces[0].shape[1]), BF16),
        scratch_shapes=[pltpu.SemaphoreType.DMA((16,))],
        compiler_params=pltpu.CompilerParams(vmem_limit_bytes=MIB),
    )(order, *pieces)


def masked_store(out, grad, mask, first, block):
    wide = row_mask(mask, out.shape[1], first, block)
    for i in range(mask.shape[0]):
        at = pl.ds(i * block, block)
        out[at, :] = grad[i * block:(i + 1) * block] * wide[i:i + 1]


def grads_kernel(rows, n_terms, block, *refs):
    take = iter(refs)
    tokens = next(take)
    terms = [[next(take) for _ in rows] for _ in range(n_terms)]
    masks = [next(take) for _ in range(n_terms)]
    outs = [next(take) for _ in range(n_terms)]
    flipped, joined = take
    step = pl.program_id(0)

    @pl.when(step == 0)
    def _():
        for i in range(len(ORDER)):
            at = pl.ds(i * 128, 128)
            flipped[:, at] = tokens[at, :].T

    for pieces, mask, out in zip(terms, masks, outs):
        for start, piece in zip(rows, pieces):
            for i in range(0, piece.shape[0], 128):
                half = (start + i) // 128
                to = ORDER.index((half // 2, half % 2)) * 128
                joined[pl.ds(to, 128), :] = piece[pl.ds(i, 128), :]
        grad = jnp.dot(flipped[...], joined[...], preferred_element_type=F32)
        masked_store(out, grad, mask[...], step * out.shape[1], block)


def term_specs(pieces, n_terms, steps, wide):
    return [
        pl.BlockSpec((piece.shape[0], wide), functools.partial(lambda at, f: (0, at + f), term * steps))
        for term in range(n_terms)
        for piece in pieces
    ]


def weight_grads(tokens, pieces, masks, wide=256):
    rows, pieces = tuple(pieces), tuple(pieces.values())
    total, features = tokens.shape
    n_terms = len(masks)
    width = pieces[0].shape[1] // n_terms
    whole = pl.BlockSpec(memory_space=pltpu.VMEM)
    block = features // masks[0].shape[0]
    return pl.pallas_call(
        functools.partial(grads_kernel, rows, n_terms, block),
        grid=(width // wide,),
        in_specs=[whole] + term_specs(pieces, n_terms, width // wide, wide) + [whole] * n_terms,
        out_specs=[pl.BlockSpec((features, wide), lambda f: (0, f))] * n_terms,
        out_shape=[jax.ShapeDtypeStruct((features, width), F32)] * n_terms,
        scratch_shapes=[pltpu.VMEM((features, total), BF16), pltpu.VMEM((total, wide), BF16)],
        compiler_params=pltpu.CompilerParams(vmem_limit_bytes=24 * MIB),
    )(tokens, *(pieces * n_terms), *masks)


def back_kernel(rows, n_terms, steps, aliased, *refs):
    take = iter(refs)
    terms = [[next(take) for _ in rows] for _ in range(n_terms)]
    weights = [next(take) for _ in range(n_terms)]
    for _ in range(aliased):
        next(take)
    keep, give, acc, joined, sems = take
    step = pl.program_id(0)
    total = None
    for pieces, weight in zip(terms, weights):
        at = 0
        for piece in pieces:
            joined[pl.ds(at, piece.shape[0]), :] = piece[...]
            at += piece.shape[0]
        part = lax.dot_general(
            joined[...], weight[...], (((1,), (1,)), ((), ())), preferred_element_type=F32
        )
        total = part if total is None else total + part

    @pl.when(step == 0)
    def _():
        acc[...] = total

    @pl.when(step > 0)
    def _():
        acc[...] += total

    @pl.when(step == steps - 1)
    def _():
        first, second = my_place()
        copies = []
        at = 0
        for start, piece in zip(rows, terms[0]):
            for row in range(start, start + piece.shape[0], 64):
                big = lax.rem(first + row // 256, SIDE)
                small = lax.rem(second + row % 256 // 64, SIDE) * 64
                for out, base in ((keep, 0), (give, 2)):
                    to = pl.multiple_of(lax.rem(big, 2) * 256 + small, 64)
                    copy = pltpu.make_async_copy(
                        acc.at[pl.ds(at, 64), :], out.at[pl.ds(to, 64), :], sems.at[at // 64]
                    )
                    copies.append((jnp.logical_and(big >= base, big < base + 2), copy))
                at += 64
        for here, copy in copies:
            pl.when(here)(copy.start)
        for here, copy in copies:
            pl.when(here)(copy.wait)


def back_product(pieces, weights, n_terms, into=(), wide=256):
    rows, pieces = tuple(pieces), tuple(pieces.values())
    features = weights.shape[0]
    width = weights.shape[1] // n_terms
    total = sum(p.shape[0] for p in pieces)
    steps = width // wide
    n_in = n_terms * (len(pieces) + 1)
    return pl.pallas_call(
        functools.partial(back_kernel, rows, n_terms, steps, len(into)),
        grid=(steps,),
        in_specs=term_specs(pieces, n_terms, steps, wide)
        + term_specs([weights], n_terms, steps, wide)
        + [pl.BlockSpec(memory_space=pl.ANY)] * len(into),
        out_specs=[pl.BlockSpec(memory_space=pl.ANY)] * 2,
        out_shape=[jax.ShapeDtypeStruct((512, features), F32)] * 2,
        scratch_shapes=[
            pltpu.VMEM((total, features), F32),
            pltpu.VMEM((total, wide), BF16),
            pltpu.SemaphoreType.DMA((total // 64,)),
        ],
        input_output_aliases={n_in + i: i for i in range(len(into))},
        compiler_params=pltpu.CompilerParams(vmem_limit_bytes=24 * MIB),
    )(*(pieces * n_terms), *([weights] * n_terms), *into)


def partial(tokens, weight):
    return jnp.dot(tokens, weight, preferred_element_type=F32) * SCALE


def sum_first(tokens, weight):
    from_left = send(partial(tokens[:256], weight).astype(F16), "first", 1)
    from_right = send(partial(tokens[256:512], weight).astype(F16), "first", -1)
    low = (partial(tokens[512:640], weight) + from_left[:128].astype(F32)).astype(F16)
    low_left = send(low, "first", 1)
    high = (partial(tokens[640:768], weight) + from_right[:128].astype(F32)).astype(F16)
    high_right = send(high, "first", -1)
    low = partial(tokens[768:896], weight) + from_right[128:].astype(F32) + low_left.astype(F32)
    low = low.astype(F16)
    high = partial(tokens[896:], weight) + from_left[128:].astype(F32) + high_right.astype(F32)
    high = high.astype(F16)
    return low, high


def sum_second(low, high):
    got = [send(values, "second", shift) for shift, values in ((1, low[64:]), (3, high[64:]), (2, high[:64]))]
    total = low[:64].astype(F32)
    for values in got:
        total = total + values.astype(F32)
    return total * (1.0 / SCALE)


def gather_second(values):
    got = {shift: send(values, "second", -shift) for shift in (1, 3, 2)}
    return jnp.concatenate([values, got[1]], axis=0), jnp.concatenate([got[2], got[3]], axis=0)


def gather_first(low, high):
    mine = jnp.concatenate([low, high], axis=0)
    left, right = send(mine, "first", 1), send(mine, "first", -1)
    far_low = send(left[:128], "first", 1)
    far_high = send(right[128:], "first", -1)
    return {0: mine, 256: right, 512: far_low, 640: far_high, 768: left}


def gather_first_halves(low, high):
    left_low, right_high = send(low, "first", 1), send(high, "first", -1)
    left_high, right_low = send(high, "first", 1), send(low, "first", -1)
    far_low = send(left_low, "first", 1)
    far_high = send(right_high, "first", -1)
    early = {0: low, 128: high, 256: right_low, 384: right_high, 768: left_low, 896: left_high}
    return early, {512: far_low, 640: far_high}


def gather_tokens(own):
    mine = {0: own}
    for shift in (1, 3, 2):
        mine[shift] = send(own, "z", -shift)
    theirs = {shift: send(mine[shift], "core", 1) for shift in (0, 1, 3, 2)}
    return [mine[i] for i in range(SIDE)] + [theirs[i] for i in range(SIDE)]


def sum_tokens(keep, give):
    chip = (keep + send(give, "core", 1)).reshape(SIDE, 128, keep.shape[1])
    total = chip[0]
    for shift in (1, 3, 2):
        total = total + send(chip[shift].astype(BF16), "z", shift).astype(F32)
    return total


def per_device(
    tokens, out_grad, gate_weight, up_weight, down_weight, gate_mask, up_mask, down_mask
):
    w_gate_up, w_down = mask_weights((gate_weight, up_weight, down_weight), (gate_mask, up_mask, down_mask))
    width = w_down.shape[1]

    ins = roll_tokens(gather_tokens(tokens))
    outs = roll_tokens(gather_tokens(out_grad))
    near_gate_up = sum_first(ins, w_gate_up)
    near_grad = sum_first(outs, w_down)

    gate_up = sum_second(*near_gate_up)
    gate, up = gate_up[:, :width], gate_up[:, width:]
    hidden = gather_first(*gather_second((gate * jax.nn.sigmoid(gate) * up).astype(BF16)))

    grad = sum_second(*near_grad)
    gate, up, grad = lax.optimization_barrier((gate, up, grad))
    sig = jax.nn.sigmoid(gate)
    act = gate * sig
    gate_term = (grad * up * sig * (1.0 + gate * (1.0 - sig))).astype(BF16)
    up_term = (grad * act).astype(BF16)
    terms = gather_second(jnp.concatenate([gate_term, up_term], axis=1))
    early, late = gather_first_halves(*terms)

    parts = back_product(hidden, w_down, 1)
    output = sum_tokens(*parts)
    (down_grad,) = weight_grads(outs, hidden, [down_mask])
    parts = back_product(early, w_gate_up, 2)
    parts = back_product(late, w_gate_up, 2, parts)
    in_grad = sum_tokens(*parts)
    gate_grad, up_grad = weight_grads(ins, early | late, [gate_mask, up_mask])
    return (output, in_grad, gate_grad, up_grad, down_grad)


def solution(mesh):
    data, weight = P(("col", "depth"), "row"), P("row", ("col", "depth"))

    return jax.shard_map(
        per_device,
        mesh=mesh,
        in_specs=(data,) * 2 + (weight,) * 6,
        out_specs=(data,) * 2 + (weight,) * 3,
        check_vma=False,
    )
```

```python
import functools

import jax
import jax.numpy as jnp
from jax import lax
from jax.experimental import pallas as pl
from jax.experimental.pallas import tpu as pltpu
from jax.sharding import PartitionSpec as P


BF16 = jnp.bfloat16
F16 = jnp.float16
F32 = jnp.float32
SIDE = 4
SCALE = 16.0
MIB = 1 << 20
MASK_VMEM = 51


def send(values, axis, shift):
    if axis == "core":
        return lax.ppermute(values, "depth", [(0, 1), (1, 0)])
    if axis == "z":
        return lax.ppermute(values, "col", [(z, (z + shift) % SIDE) for z in range(SIDE)])
    perm = []
    for y in range(SIDE):
        for x in range(SIDE):
            for core in range(2):
                along_x = (core == 0) == (axis == "first")
                to_y, to_x = (y, (x + shift) % SIDE) if along_x else ((y + shift) % SIDE, x)
                perm.append(((y * SIDE + x) * 2 + core, (to_y * SIDE + to_x) * 2 + core))
    return lax.ppermute(values, ("row", "depth"), perm)


def row_mask(mask, width, first, block):
    rows = lax.broadcasted_iota(jnp.int32, (mask.shape[1], width), 0)
    cols = lax.broadcasted_iota(jnp.int32, (mask.shape[1], width), 1) + first
    spread = jnp.logical_and(cols >= rows * block, cols < (rows + 1) * block).astype(F32)
    return jnp.dot(mask.astype(F32), spread, preferred_element_type=F32)


def mask_kernel(block, *refs):
    masks, weights, (gate_up_out, down_out), (held, wide, small, came, left, sems) = refs[:3], refs[3:6], refs[6:8], refs[8:]
    count, width = masks[0].shape[0], weights[0].shape[1]
    copies = [pltpu.make_async_copy(mask, small.at[j], sems.at[j]) for j, mask in enumerate(masks)]
    for copy in copies:
        copy.start()
    outs = ((gate_up_out, 0), (gate_up_out, width), (down_out, 0))

    def read(i, j):
        at = pl.ds(pl.multiple_of(i * block, block), block)
        return pltpu.make_async_copy(weights[j].at[at, :], held.at[j, at, :], came.at[j, i])

    def write(i, j):
        at = pl.ds(pl.multiple_of(i * block, block), block)
        out, first = outs[j]
        return pltpu.make_async_copy(held.at[j, at, :], out.at[at, pl.ds(first, width)], left.at[j, i])

    def every(act):
        @pl.loop(0, count)
        def _(i):
            for j in range(3):
                act(i, j)

    every(lambda i, j: read(i, j).start())
    for j, copy in enumerate(copies):
        copy.wait()
        wide[j] = row_mask(small[j], width, 0, block)

    def apply(i, j):
        read(i, j).wait()
        at = pl.ds(pl.multiple_of(i * block, block), block)
        held[j, at, :] = (held[j, at, :].astype(F32) * wide[j, pl.ds(i, 1), :]).astype(BF16)
        write(i, j).start()

    every(apply)
    every(lambda i, j: write(i, j).wait())


def mask_weights(weights, masks):
    rows, width = weights[0].shape
    count = masks[0].shape[0]
    return pl.pallas_call(
        functools.partial(mask_kernel, rows // count),
        in_specs=[pl.BlockSpec(memory_space=pl.ANY)] * 6,
        out_specs=[pl.BlockSpec(memory_space=pl.ANY)] * 2,
        out_shape=[jax.ShapeDtypeStruct((rows, 2 * width), BF16), jax.ShapeDtypeStruct((rows, width), BF16)],
        scratch_shapes=[
            pltpu.VMEM((3, rows, width), BF16),
            pltpu.VMEM((3, count, width), F32),
            pltpu.VMEM((3,) + masks[0].shape, jnp.int32),
            pltpu.SemaphoreType.DMA((3, count)),
            pltpu.SemaphoreType.DMA((3, count)),
            pltpu.SemaphoreType.DMA((3,)),
        ],
        compiler_params=pltpu.CompilerParams(vmem_limit_bytes=MASK_VMEM * MIB),
        name="mask_weights",
    )(*masks, *weights)


def token_row(near, far):
    row, core = lax.axis_index("row"), lax.axis_index("depth")
    y, x = row // SIDE, lax.rem(row, SIDE)
    to_x = lax.rem(x + jnp.where(core == 0, near, far), SIDE)
    to_y = lax.rem(y + jnp.where(core == 0, far, near), SIDE)
    return pl.multiple_of((to_x * SIDE + to_y) * 8, 8)


def roll_kernel(*refs):
    *pairs, sems = refs
    half = len(pairs) // 2
    copies = []
    for i in range(16):
        start = token_row(i // SIDE, i % SIDE)
        for j in range(half):
            copy = pltpu.make_async_copy(
                pairs[j].at[pl.ds(start, 8), :], pairs[half + j].at[pl.ds(i * 8, 8), :], sems.at[j, i]
            )
            copy.start()
            copies.append(copy)
    for copy in copies:
        copy.wait()


def roll_own(*arrays):
    return pl.pallas_call(
        roll_kernel,
        in_specs=[pl.BlockSpec(memory_space=pl.ANY)] * len(arrays),
        out_specs=[pl.BlockSpec(memory_space=pl.ANY)] * len(arrays),
        out_shape=[jax.ShapeDtypeStruct(a.shape, a.dtype) for a in arrays],
        scratch_shapes=[pltpu.SemaphoreType.DMA((len(arrays), 16))],
        compiler_params=pltpu.CompilerParams(vmem_limit_bytes=60 * MIB),
        name="roll_own",
    )(*arrays)


def unroll_kernel(own, *refs):
    *got, out = refs
    total = own[...]
    for ref in got:
        total = total + ref[...].astype(F32)
    for i in range(16):
        out[pl.ds(token_row(i // SIDE, i % SIDE), 8), :] = total[i * 8:(i + 1) * 8]


def unroll_sum(own, got):
    whole = pl.BlockSpec(memory_space=pltpu.VMEM)
    return pl.pallas_call(
        unroll_kernel,
        in_specs=[whole] * (1 + len(got)),
        out_specs=whole,
        out_shape=jax.ShapeDtypeStruct(own.shape, F32),
        compiler_params=pltpu.CompilerParams(vmem_limit_bytes=4 * MIB),
        name="unroll_sum",
    )(own, *got)


def place_kernel(*refs):
    *pieces, out, sems = refs
    copies = []
    for i, piece in enumerate(pieces):
        if i < SIDE:
            copies.append(pltpu.make_async_copy(piece, out.at[:, :, i], sems.at[i]))
            continue
        for near in range(SIDE):
            at = sems.at[SIDE + (i - SIDE) * SIDE + near]
            copies.append(pltpu.make_async_copy(piece.at[:, near], out.at[near, :, i], at))
    for copy in copies:
        copy.start()
    for copy in copies:
        copy.wait()


def place_tokens(pieces):
    features = pieces[0].shape[1]
    out = pl.pallas_call(
        place_kernel,
        in_specs=[pl.BlockSpec(memory_space=pl.ANY)] * len(pieces),
        out_specs=pl.BlockSpec(memory_space=pl.ANY),
        out_shape=jax.ShapeDtypeStruct((SIDE, SIDE, len(pieces), 8, features), BF16),
        scratch_shapes=[pltpu.SemaphoreType.DMA((SIDE + SIDE * SIDE,))],
        compiler_params=pltpu.CompilerParams(vmem_limit_bytes=MIB),
    )(*[p.reshape(SIDE, SIDE, 8, features) for p in pieces])
    return out.reshape(128 * len(pieces), features)


def masked_store(out, grad, mask, first, block):
    wide = row_mask(mask, out.shape[1], first, block)
    for i in range(mask.shape[0]):
        at = pl.ds(i * block, block)
        out[at, :] = grad[i * block:(i + 1) * block] * wide[i:i + 1]


def grads_kernel(n_pieces, n_terms, block, *refs):
    take = iter(refs)
    tokens = next(take)
    terms = [[next(take) for _ in range(n_pieces)] for _ in range(n_terms)]
    masks = [next(take) for _ in range(n_terms)]
    outs = [next(take) for _ in range(n_terms)]
    flipped, joined = take
    step = pl.program_id(0)

    @pl.when(step == 0)
    def _():
        @pl.loop(0, tokens.shape[0] // 128)
        def _(i):
            at = pl.ds(pl.multiple_of(i * 128, 128), 128)
            flipped[:, at] = tokens[at, :].T

    for pieces, mask, out in zip(terms, masks, outs):
        at = 0
        for piece in pieces:
            joined[pl.ds(at, piece.shape[0]), :] = piece[...]
            at += piece.shape[0]
        grad = jnp.dot(flipped[...], joined[...], preferred_element_type=F32)
        masked_store(out, grad, mask[...], step * out.shape[1], block)


def weight_grads(tokens, pieces, masks, wide=256):
    total, features = tokens.shape
    n_terms = len(masks)
    width = pieces[0].shape[1] // n_terms
    steps = width // wide
    whole = pl.BlockSpec(memory_space=pltpu.VMEM)
    block = features // masks[0].shape[0]
    term_specs = [
        pl.BlockSpec((piece.shape[0], wide), functools.partial(lambda at, f: (0, at + f), term * steps))
        for term in range(n_terms)
        for piece in pieces
    ]
    return pl.pallas_call(
        functools.partial(grads_kernel, len(pieces), n_terms, block),
        grid=(steps,),
        in_specs=[whole] + term_specs + [whole] * n_terms,
        out_specs=[pl.BlockSpec((features, wide), lambda f: (0, f))] * n_terms,
        out_shape=[jax.ShapeDtypeStruct((features, width), F32)] * n_terms,
        scratch_shapes=[pltpu.VMEM((features, total), BF16), pltpu.VMEM((total, wide), BF16)],
        compiler_params=pltpu.CompilerParams(vmem_limit_bytes=24 * MIB),
    )(tokens, *(list(pieces) * n_terms), *masks)


def partial(tokens, weight):
    return jnp.dot(tokens, weight, preferred_element_type=F32) * SCALE


def sum_first(tokens, weight):
    from_left = send(partial(tokens[384:640], weight).astype(F16), "first", 1)
    from_right = send(partial(tokens[640:896], weight).astype(F16), "first", -1)
    low = (partial(tokens[256:384], weight) + from_left[128:].astype(F32)).astype(F16)
    low_left = send(low, "first", 1)
    high = (partial(tokens[896:], weight) + from_right[:128].astype(F32)).astype(F16)
    high_right = send(high, "first", -1)
    low = partial(tokens[:128], weight) + from_right[128:].astype(F32) + low_left.astype(F32)
    low = low.astype(F16)
    high = partial(tokens[128:256], weight) + from_left[:128].astype(F32) + high_right.astype(F32)
    high = high.astype(F16)
    return low, high


def sum_second(low, high):
    got = [send(values, "second", shift) for shift, values in ((1, low[64:]), (3, high[64:]), (2, high[:64]))]
    total = low[:64].astype(F32)
    for values in got:
        total = total + values.astype(F32)
    return total * (1.0 / SCALE)


def gather_second(values):
    got = {shift: send(values, "second", -shift) for shift in (1, 3, 2)}
    return jnp.concatenate([values, got[1]], axis=0), jnp.concatenate([got[2], got[3]], axis=0)


def gather_first(low, high):
    mine = jnp.concatenate([low, high], axis=0)
    left, right = send(mine, "first", 1), send(mine, "first", -1)
    far_low = send(left[:128], "first", 1)
    far_high = send(right[128:], "first", -1)
    return [mine, right, far_low, far_high, left]


def gather_first_halves(low, high):
    left_low, right_high = send(low, "first", 1), send(high, "first", -1)
    left_high, right_low = send(high, "first", 1), send(low, "first", -1)
    far_low = send(left_low, "first", 1)
    far_high = send(right_high, "first", -1)
    return [low, high, right_low, right_high, far_low, far_high, left_low, left_high]


def gather_tokens(own):
    mine = {0: own}
    for shift in (1, 3, 2):
        mine[shift] = send(own, "z", -shift)
    theirs = {shift: send(mine[shift], "core", 1) for shift in (0, 1, 3, 2)}
    return place_tokens([mine[i] for i in range(SIDE)] + [theirs[i] for i in range(SIDE)])


def chip_kernel(sizes, *refs):
    count = len(sizes)
    mine, theirs, (own, *outs), (kept, came, sems) = refs[:count], refs[count:2 * count], refs[2 * count:-3], refs[-3:]
    copies = []
    at = 0
    for i, size in enumerate(sizes):
        to = pl.ds(at, size)
        copies.append(pltpu.make_async_copy(mine[i].at[:, 0], kept.at[to], sems.at[0, i]))
        copies.append(pltpu.make_async_copy(theirs[i].at[:, 1], came.at[to], sems.at[1, i]))
        at += size
    for copy in copies:
        copy.start()
    for copy in copies:
        copy.wait()

    @pl.loop(0, SIDE)
    def _(near):
        for far in range(SIDE):
            total = kept[near * SIDE + far] + came[far * SIDE + near]
            at = pl.ds(pl.multiple_of((near * SIDE + far) * 8, 8), 8)
            own[at, :] = total[:8]
            for z, out in enumerate(outs):
                out[at, :] = total[(z + 1) * 8:(z + 2) * 8].astype(BF16)


def chip_sum(mine, theirs):
    features = mine[0].shape[1]
    sizes = tuple(p.shape[0] // 64 for p in mine)
    shape = (sum(p.shape[0] for p in mine) // 8, features)
    whole = pl.BlockSpec(memory_space=pltpu.VMEM)
    return pl.pallas_call(
        functools.partial(chip_kernel, sizes),
        in_specs=[pl.BlockSpec(memory_space=pl.ANY)] * (2 * len(sizes)),
        out_specs=[whole] * SIDE,
        out_shape=[jax.ShapeDtypeStruct(shape, F32)] + [jax.ShapeDtypeStruct(shape, BF16)] * (SIDE - 1),
        scratch_shapes=[pltpu.VMEM((16, 32, features), F32)] * 2 + [pltpu.SemaphoreType.DMA((2, len(sizes)))],
        compiler_params=pltpu.CompilerParams(vmem_limit_bytes=6 * MIB),
        name="chip_sum",
    )(*[p.reshape(-1, 2, 32, features) for p in (*mine, *theirs)])


def back_product(groups, weights):
    mine, theirs = [], []
    for pieces in groups:
        parts = [
            lax.dot_general(p, weights, (((1,), (1,)), ((), ())), preferred_element_type=F32) for p in pieces
        ]
        mine.append(jnp.concatenate(parts, axis=0))
        theirs.append(send(mine[-1], "core", 1))
    own, *parts = chip_sum(mine, theirs)
    return unroll_sum(own, [send(parts[z - 1], "z", z) for z in (1, 3, 2)])


def per_device(
    tokens, out_grad, gate_weight, up_weight, down_weight, gate_mask, up_mask, down_mask
):
    tokens, out_grad = roll_own(tokens, out_grad)
    w_gate_up, w_down = mask_weights((gate_weight, up_weight, down_weight), (gate_mask, up_mask, down_mask))
    width = w_down.shape[1]

    ins = gather_tokens(tokens)
    outs = gather_tokens(out_grad)
    near_gate_up = sum_first(ins, w_gate_up)
    near_grad = sum_first(outs, w_down)

    gate_up = sum_second(*near_gate_up)
    gate, up = gate_up[:, :width], gate_up[:, width:]
    hidden = gather_first(*gather_second((gate * jax.nn.sigmoid(gate) * up).astype(BF16)))

    grad = sum_second(*near_grad)
    gate, up, grad = lax.optimization_barrier((gate, up, grad))
    sig = jax.nn.sigmoid(gate)
    act = gate * sig
    gate_term = (grad * up * sig * (1.0 + gate * (1.0 - sig))).astype(BF16)
    up_term = (grad * act).astype(BF16)
    terms = gather_second(jnp.concatenate([gate_term, up_term], axis=1))
    terms = gather_first_halves(*terms)

    output = back_product([hidden], w_down)
    (down_grad,) = weight_grads(outs, hidden, [down_mask])
    in_grad = back_product([terms[i:i + 2] for i in range(0, 8, 2)], w_gate_up)
    gate_grad, up_grad = weight_grads(ins, terms, [gate_mask, up_mask])
    return (output, in_grad, gate_grad, up_grad, down_grad)


def solution(mesh):
    data, weight = P(("col", "depth"), "row"), P("row", ("col", "depth"))

    return jax.shard_map(
        per_device,
        mesh=mesh,
        in_specs=(data,) * 2 + (weight,) * 6,
        out_specs=(data,) * 2 + (weight,) * 3,
        check_vma=False,
    )
```

```python
import functools

import jax
import jax.numpy as jnp
from jax import lax
from jax.experimental import pallas as pl
from jax.experimental.pallas import tpu as pltpu
from jax.sharding import PartitionSpec as P


BF16 = jnp.bfloat16
F16 = jnp.float16
F32 = jnp.float32
SIDE = 4
SCALE = 16.0
MIB = 1 << 20


def send(values, axis, shift):
    if axis == "core":
        return lax.ppermute(values, "depth", [(0, 1), (1, 0)])
    if axis == "z":
        return lax.ppermute(values, "col", [(z, (z + shift) % SIDE) for z in range(SIDE)])
    perm = []
    for y in range(SIDE):
        for x in range(SIDE):
            for core in range(2):
                along_x = (core == 0) == (axis == "first")
                to_y, to_x = (y, (x + shift) % SIDE) if along_x else ((y + shift) % SIDE, x)
                perm.append(((y * SIDE + x) * 2 + core, (to_y * SIDE + to_x) * 2 + core))
    return lax.ppermute(values, ("row", "depth"), perm)


def row_mask(mask, width, first, block):
    rows = lax.broadcasted_iota(jnp.int32, (mask.shape[1], width), 0)
    cols = lax.broadcasted_iota(jnp.int32, (mask.shape[1], width), 1) + first
    spread = jnp.logical_and(cols >= rows * block, cols < (rows + 1) * block).astype(F32)
    return jnp.dot(mask.astype(F32), spread, preferred_element_type=F32)


def mask_kernel(block, count, *refs):
    masks, weights, out, (held, wide, small, came, left, sems) = refs[:count], refs[count:-7], refs[-7], refs[-6:]
    rows, width = weights[0].shape
    copies = [pltpu.make_async_copy(mask, small.at[j], sems.at[j]) for j, mask in enumerate(masks)]
    for copy in copies:
        copy.start()

    def read(i, j):
        at = pl.ds(pl.multiple_of(i * block, block), block)
        return pltpu.make_async_copy(weights[j].at[at, :], held.at[j, at, :], came.at[j, i])

    def write(i, j):
        at = pl.ds(pl.multiple_of(i * block, block), block)
        return pltpu.make_async_copy(held.at[j, at, :], out.at[at, pl.ds(j * width, width)], left.at[j, i])

    def every(act):
        @pl.loop(0, rows // block)
        def _(i):
            for j in range(count):
                act(i, j)

    every(lambda i, j: read(i, j).start())
    for j, copy in enumerate(copies):
        copy.wait()
        wide[j] = row_mask(small[j], width, 0, block)

    def apply(i, j):
        read(i, j).wait()
        at = pl.ds(pl.multiple_of(i * block, block), block)
        held[j, at, :] = (held[j, at, :].astype(F32) * wide[j, pl.ds(i, 1), :]).astype(BF16)
        write(i, j).start()

    every(apply)
    every(lambda i, j: write(i, j).wait())


def mask_weights(weights, masks, vmem):
    rows, width = weights[0].shape
    count, blocks = len(weights), masks[0].shape[0]
    return pl.pallas_call(
        functools.partial(mask_kernel, rows // blocks, count),
        in_specs=[pl.BlockSpec(memory_space=pl.ANY)] * (2 * count),
        out_specs=pl.BlockSpec(memory_space=pl.ANY),
        out_shape=jax.ShapeDtypeStruct((rows, count * width), BF16),
        scratch_shapes=[
            pltpu.VMEM((count, rows, width), BF16),
            pltpu.VMEM((count, blocks, width), F32),
            pltpu.VMEM((count,) + masks[0].shape, jnp.int32),
            pltpu.SemaphoreType.DMA((count, blocks)),
            pltpu.SemaphoreType.DMA((count, blocks)),
            pltpu.SemaphoreType.DMA((count,)),
        ],
        compiler_params=pltpu.CompilerParams(vmem_limit_bytes=vmem * MIB),
    )(*masks, *weights)


def token_row(near, far):
    row, core = lax.axis_index("row"), lax.axis_index("depth")
    y, x = row // SIDE, lax.rem(row, SIDE)
    to_x = lax.rem(x + jnp.where(core == 0, near, far), SIDE)
    to_y = lax.rem(y + jnp.where(core == 0, far, near), SIDE)
    return pl.multiple_of((to_x * SIDE + to_y) * 8, 8)


def roll_kernel(*refs):
    half = len(refs) // 2
    for i in range(16):
        start = token_row(i // SIDE, i % SIDE)
        for j in range(half):
            refs[half + j][pl.ds(i * 8, 8), :] = refs[j][pl.ds(start, 8), :]


def roll_own(*arrays):
    whole = pl.BlockSpec(memory_space=pltpu.VMEM)
    return pl.pallas_call(
        roll_kernel,
        in_specs=[whole] * len(arrays),
        out_specs=[whole] * len(arrays),
        out_shape=[jax.ShapeDtypeStruct(a.shape, a.dtype) for a in arrays],
        compiler_params=pltpu.CompilerParams(vmem_limit_bytes=60 * MIB),
        name="roll_own",
    )(*arrays)


def unroll_kernel(count, *refs):
    owns, got, outs = refs[:count], refs[count:-count], refs[-count:]
    for j, (own, out) in enumerate(zip(owns, outs)):
        width = own.shape[1]
        total = own[...]
        for ref in got:
            total = total + ref[:, pl.ds(j * width, width)].astype(F32)
        for i in range(16):
            out[pl.ds(token_row(i // SIDE, i % SIDE), 8), :] = total[i * 8:(i + 1) * 8]


def unroll_sum(owns, got):
    whole = pl.BlockSpec(memory_space=pltpu.VMEM)
    return pl.pallas_call(
        functools.partial(unroll_kernel, len(owns)),
        in_specs=[whole] * (len(owns) + len(got)),
        out_specs=[whole] * len(owns),
        out_shape=[jax.ShapeDtypeStruct(own.shape, F32) for own in owns],
        compiler_params=pltpu.CompilerParams(vmem_limit_bytes=6 * MIB),
        name="unroll_sum",
    )(*owns, *got)


def place_kernel(*refs):
    *pieces, out, sems = refs
    copies = []
    for i, piece in enumerate(pieces):
        if i < SIDE:
            copies.append(pltpu.make_async_copy(piece, out.at[:, :, i], sems.at[i]))
            continue
        for near in range(SIDE):
            at = sems.at[SIDE + (i - SIDE) * SIDE + near]
            copies.append(pltpu.make_async_copy(piece.at[:, near], out.at[near, :, i], at))
    for copy in copies:
        copy.start()
    for copy in copies:
        copy.wait()


def place_tokens(pieces):
    features = pieces[0].shape[1]
    out = pl.pallas_call(
        place_kernel,
        in_specs=[pl.BlockSpec(memory_space=pl.ANY)] * len(pieces),
        out_specs=pl.BlockSpec(memory_space=pl.ANY),
        out_shape=jax.ShapeDtypeStruct((SIDE, SIDE, len(pieces), 8, features), BF16),
        scratch_shapes=[pltpu.SemaphoreType.DMA((SIDE + SIDE * SIDE,))],
        compiler_params=pltpu.CompilerParams(vmem_limit_bytes=MIB),
    )(*[p.reshape(SIDE, SIDE, 8, features) for p in pieces])
    return out.reshape(128 * len(pieces), features)


def masked_store(out, grad, mask, first, block):
    wide = row_mask(mask, out.shape[1], first, block)
    for i in range(mask.shape[0]):
        at = pl.ds(i * block, block)
        out[at, :] = grad[i * block:(i + 1) * block] * wide[i:i + 1]


def grads_kernel(n_pieces, n_terms, block, *refs):
    take = iter(refs)
    flipped = next(take)
    terms = [[next(take) for _ in range(n_pieces)] for _ in range(n_terms)]
    masks = [next(take) for _ in range(n_terms)]
    outs = [next(take) for _ in range(n_terms)]
    (joined,) = take
    step = pl.program_id(0)

    for pieces, mask, out in zip(terms, masks, outs):
        at = 0
        for piece in pieces:
            joined[pl.ds(at, piece.shape[0]), :] = piece[...]
            at += piece.shape[0]
        grad = jnp.dot(flipped[...], joined[...], preferred_element_type=F32)
        masked_store(out, grad, mask[...], step * out.shape[1], block)


def flip_kernel(tokens, out):
    @pl.loop(0, tokens.shape[0] // 128)
    def _(i):
        at = pl.ds(pl.multiple_of(i * 128, 128), 128)
        out[:, at] = tokens[at, :].T


def flip(tokens):
    return pl.pallas_call(
        flip_kernel,
        in_specs=[pl.BlockSpec(memory_space=pltpu.VMEM)],
        out_specs=pl.BlockSpec(memory_space=pltpu.VMEM),
        out_shape=jax.ShapeDtypeStruct(tokens.shape[::-1], tokens.dtype),
        compiler_params=pltpu.CompilerParams(vmem_limit_bytes=6 * MIB),
    )(tokens)


def weight_grads(flipped, pieces, masks, wide=256):
    features, total = flipped.shape
    n_terms = len(masks)
    width = pieces[0].shape[1] // n_terms
    steps = width // wide
    whole = pl.BlockSpec(memory_space=pltpu.VMEM)
    block = features // masks[0].shape[0]
    term_specs = [
        pl.BlockSpec((piece.shape[0], wide), functools.partial(lambda at, f: (0, at + f), term * steps))
        for term in range(n_terms)
        for piece in pieces
    ]
    return pl.pallas_call(
        functools.partial(grads_kernel, len(pieces), n_terms, block),
        grid=(steps,),
        in_specs=[whole] + term_specs + [whole] * n_terms,
        out_specs=[pl.BlockSpec((features, wide), lambda f: (0, f))] * n_terms,
        out_shape=[jax.ShapeDtypeStruct((features, width), F32)] * n_terms,
        scratch_shapes=[pltpu.VMEM((total, wide), BF16)],
        compiler_params=pltpu.CompilerParams(vmem_limit_bytes=24 * MIB),
    )(flipped, *(list(pieces) * n_terms), *masks)


def partial(tokens, weight):
    return jnp.dot(tokens, weight, preferred_element_type=F32) * SCALE


def sum_first(tokens, weight):
    from_left = send(partial(tokens[384:640], weight).astype(F16), "first", 1)
    from_right = send(partial(tokens[640:896], weight).astype(F16), "first", -1)
    low = (partial(tokens[256:384], weight) + from_left[128:].astype(F32)).astype(F16)
    low_left = send(low, "first", 1)
    high = (partial(tokens[896:], weight) + from_right[:128].astype(F32)).astype(F16)
    high_right = send(high, "first", -1)
    low = partial(tokens[:128], weight) + from_right[128:].astype(F32) + low_left.astype(F32)
    low = low.astype(F16)
    high = partial(tokens[128:256], weight) + from_left[:128].astype(F32) + high_right.astype(F32)
    high = high.astype(F16)
    return low, high


def sum_second(low, high):
    got = [send(values, "second", shift) for shift, values in ((1, low[64:]), (3, high[64:]), (2, high[:64]))]
    total = low[:64].astype(F32)
    for values in got:
        total = total + values.astype(F32)
    return total * (1.0 / SCALE)


def gather_second(values):
    got = {shift: send(values, "second", -shift) for shift in (1, 3, 2)}
    return jnp.concatenate([values, got[1]], axis=0), jnp.concatenate([got[2], got[3]], axis=0)


def gather_first(low, high):
    mine = jnp.concatenate([low, high], axis=0)
    left, right = send(mine, "first", 1), send(mine, "first", -1)
    far_low = send(left[:128], "first", 1)
    far_high = send(right[128:], "first", -1)
    return [mine, right, far_low, far_high, left]


def gather_first_halves(low, high):
    left_low, right_high = send(low, "first", 1), send(high, "first", -1)
    left_high, right_low = send(high, "first", 1), send(low, "first", -1)
    far_low = send(left_low, "first", 1)
    far_high = send(right_high, "first", -1)
    return [low, high, right_low, right_high, far_low, far_high, left_low, left_high]


def gather_tokens(own):
    mine = {0: own}
    for shift in (1, 3, 2):
        mine[shift] = send(own, "z", -shift)
    theirs = {shift: send(mine[shift], "core", 1) for shift in (0, 1, 3, 2)}
    return place_tokens([mine[i] for i in range(SIDE)] + [theirs[i] for i in range(SIDE)])


def chip_kernel(sizes, *refs):
    count = len(sizes)
    mine, theirs, (own, *outs), (kept, came, sems) = refs[:count], refs[count:2 * count], refs[2 * count:-3], refs[-3:]
    copies = []
    at = 0
    for i, size in enumerate(sizes):
        to = pl.ds(at, size)
        copies.append(pltpu.make_async_copy(mine[i].at[:, 0], kept.at[to], sems.at[0, i]))
        copies.append(pltpu.make_async_copy(theirs[i].at[:, 1], came.at[to], sems.at[1, i]))
        at += size
    for copy in copies:
        copy.start()
    for copy in copies:
        copy.wait()

    @pl.loop(0, SIDE)
    def _(near):
        for far in range(SIDE):
            total = kept[near * SIDE + far] + came[far * SIDE + near]
            at = pl.ds(pl.multiple_of((near * SIDE + far) * 8, 8), 8)
            own[at, :] = total[:8]
            for z, out in enumerate(outs):
                out[at, :] = total[(z + 1) * 8:(z + 2) * 8].astype(BF16)


def chip_sum(mine, theirs):
    features = mine[0].shape[1]
    sizes = tuple(p.shape[0] // 64 for p in mine)
    shape = (sum(p.shape[0] for p in mine) // 8, features)
    whole = pl.BlockSpec(memory_space=pltpu.VMEM)
    return pl.pallas_call(
        functools.partial(chip_kernel, sizes),
        in_specs=[pl.BlockSpec(memory_space=pl.ANY)] * (2 * len(sizes)),
        out_specs=[whole] * SIDE,
        out_shape=[jax.ShapeDtypeStruct(shape, F32)] + [jax.ShapeDtypeStruct(shape, BF16)] * (SIDE - 1),
        scratch_shapes=[pltpu.VMEM((16, 32, features), F32)] * 2 + [pltpu.SemaphoreType.DMA((2, len(sizes)))],
        compiler_params=pltpu.CompilerParams(vmem_limit_bytes=6 * MIB),
        name="chip_sum",
    )(*[p.reshape(-1, 2, 32, features) for p in (*mine, *theirs)])


def back_product(groups, weights):
    mine, theirs = [], []
    for pieces in groups:
        parts = [
            lax.dot_general(p, weights, (((1,), (1,)), ((), ())), preferred_element_type=F32) for p in pieces
        ]
        mine.append(jnp.concatenate(parts, axis=0))
        theirs.append(send(mine[-1], "core", 1))
    return chip_sum(mine, theirs)


def per_device(
    tokens, out_grad, gate_weight, up_weight, down_weight, gate_mask, up_mask, down_mask
):
    tokens, out_grad = roll_own(tokens, out_grad)
    w_gate_up = mask_weights((gate_weight, up_weight), (gate_mask, up_mask), 54)
    w_down = mask_weights((down_weight,), (down_mask,), 40)
    width = w_down.shape[1]

    ins = gather_tokens(tokens)
    outs = gather_tokens(out_grad)
    near_gate_up = sum_first(ins, w_gate_up)
    near_grad = sum_first(outs, w_down)

    gate_up = sum_second(*near_gate_up)
    gate, up = gate_up[:, :width], gate_up[:, width:]
    hidden = gather_first(*gather_second((gate * jax.nn.sigmoid(gate) * up).astype(BF16)))

    grad = sum_second(*near_grad)
    gate, up, grad = lax.optimization_barrier((gate, up, grad))
    sig = jax.nn.sigmoid(gate)
    act = gate * sig
    gate_term = (grad * up * sig * (1.0 + gate * (1.0 - sig))).astype(BF16)
    up_term = (grad * act).astype(BF16)
    terms = gather_second(jnp.concatenate([gate_term, up_term], axis=1))
    terms = gather_first_halves(*terms)

    outs_flipped = flip(outs)
    ins_flipped = flip(ins)

    ys = back_product([hidden], w_down)
    (down_grad,) = weight_grads(outs_flipped, hidden, [down_mask])
    dxs = back_product([terms[i:i + 2] for i in range(0, 8, 2)], w_gate_up)
    gate_grad, up_grad = weight_grads(ins_flipped, terms, [gate_mask, up_mask])
    got = [send(jnp.concatenate([ys[z], dxs[z]], axis=1), "z", z) for z in (1, 3, 2)]
    output, in_grad = unroll_sum((ys[0], dxs[0]), got)
    return (output, in_grad, gate_grad, up_grad, down_grad)


def solution(mesh):
    data, weight = P(("col", "depth"), "row"), P("row", ("col", "depth"))

    return jax.shard_map(
        per_device,
        mesh=mesh,
        in_specs=(data,) * 2 + (weight,) * 6,
        out_specs=(data,) * 2 + (weight,) * 3,
        check_vma=False,
    )
```

```python
import functools

import jax
import jax.numpy as jnp
from jax import lax
from jax.experimental import pallas as pl
from jax.experimental.pallas import tpu as pltpu
from jax.sharding import PartitionSpec as P


BF16 = jnp.bfloat16
F16 = jnp.float16
F32 = jnp.float32
SIDE = 4
SCALE = 16.0
MIB = 1 << 20
WIDE = 256


def send(values, axis, shift):
    if axis == "core":
        return lax.ppermute(values, "depth", [(0, 1), (1, 0)])
    if axis == "z":
        return lax.ppermute(values, "col", [(z, (z + shift) % SIDE) for z in range(SIDE)])
    perm = []
    for y in range(SIDE):
        for x in range(SIDE):
            for core in range(2):
                along_x = (core == 0) == (axis == "first")
                to_y, to_x = (y, (x + shift) % SIDE) if along_x else ((y + shift) % SIDE, x)
                perm.append(((y * SIDE + x) * 2 + core, (to_y * SIDE + to_x) * 2 + core))
    return lax.ppermute(values, ("row", "depth"), perm)


def row_mask(mask, width, first, block):
    rows = lax.broadcasted_iota(jnp.int32, (mask.shape[1], width), 0)
    cols = lax.broadcasted_iota(jnp.int32, (mask.shape[1], width), 1) + first
    spread = jnp.logical_and(cols >= rows * block, cols < (rows + 1) * block).astype(F32)
    return jnp.dot(mask.astype(F32), spread, preferred_element_type=F32)


def mask_kernel(block, count, *refs):
    masks, weights, out = refs[:count], refs[count:-1], refs[-1]
    width = weights[0].shape[1]
    for j, (mask, weight) in enumerate(zip(masks, weights)):
        wide = row_mask(jnp.broadcast_to(mask[0], (8, mask.shape[2])), width, 0, block)
        out[:, pl.ds(j * width, width)] = (weight[...].astype(F32) * wide[0:1]).astype(BF16)


def mask_weights(weights, masks, vmem):
    rows, width = weights[0].shape
    count, (mrows, mcols) = len(weights), masks[0].shape
    block = rows // mrows
    return pl.pallas_call(
        functools.partial(mask_kernel, block, count),
        grid=(mrows,),
        in_specs=[pl.BlockSpec((1, 1, mcols), lambda i: (i, 0, 0))] * count
        + [pl.BlockSpec((block, width), lambda i: (i, 0))] * count,
        out_specs=pl.BlockSpec((block, count * width), lambda i: (i, 0)),
        out_shape=jax.ShapeDtypeStruct((rows, count * width), BF16),
        compiler_params=pltpu.CompilerParams(vmem_limit_bytes=vmem * MIB),
    )(*[m.reshape(mrows, 1, mcols) for m in masks], *weights)


def token_row(near, far):
    row, core = lax.axis_index("row"), lax.axis_index("depth")
    y, x = row // SIDE, lax.rem(row, SIDE)
    to_x = lax.rem(x + jnp.where(core == 0, near, far), SIDE)
    to_y = lax.rem(y + jnp.where(core == 0, far, near), SIDE)
    return pl.multiple_of((to_x * SIDE + to_y) * 8, 8)


def unroll_kernel(own, *refs):
    *got, out = refs
    total = own[...]
    for ref in got:
        total = total + ref[...].astype(F32)
    for i in range(16):
        out[pl.ds(token_row(i // SIDE, i % SIDE), 8), :] = total[i * 8:(i + 1) * 8]


def unroll_sum(own, got):
    whole = pl.BlockSpec(memory_space=pltpu.VMEM)
    return pl.pallas_call(
        unroll_kernel,
        in_specs=[whole] * (1 + len(got)),
        out_specs=whole,
        out_shape=jax.ShapeDtypeStruct(own.shape, F32),
        compiler_params=pltpu.CompilerParams(vmem_limit_bytes=4 * MIB),
        name="unroll_sum",
    )(own, *got)


def place_kernel(*refs):
    *pieces, out = refs
    slots = [(ref, at) for ref in pieces for at in range(0, ref.shape[0], 128)]

    @pl.loop(0, SIDE)
    def _(near):
        for far in range(SIDE):
            start = token_row(near, far)
            for i, (ref, at) in enumerate(slots):
                to = pl.multiple_of((near * SIDE + far) * 64 + i * 8, 8)
                out[pl.ds(to, 8), :] = ref[pl.ds(pl.multiple_of(at + start, 8), 8), :]


def place_tokens(pieces):
    whole = pl.BlockSpec(memory_space=pltpu.VMEM)
    rows = sum(p.shape[0] for p in pieces)
    return pl.pallas_call(
        place_kernel,
        in_specs=[whole] * len(pieces),
        out_specs=whole,
        out_shape=jax.ShapeDtypeStruct((rows, pieces[0].shape[1]), BF16),
        compiler_params=pltpu.CompilerParams(vmem_limit_bytes=6 * MIB),
    )(*pieces)


def join_kernel(*refs):
    *pieces, out, sems = refs
    copies = []
    for i, piece in enumerate(pieces):
        rows = piece.shape[0]
        copies.append(pltpu.make_async_copy(piece, out.at[pl.ds(i * rows, rows), :], sems.at[i]))
    for copy in copies:
        copy.start()
    for copy in copies:
        copy.wait()


def join_rows(pieces):
    return pl.pallas_call(
        join_kernel,
        in_specs=[pl.BlockSpec(memory_space=pl.ANY)] * len(pieces),
        out_specs=pl.BlockSpec(memory_space=pl.ANY),
        out_shape=jax.ShapeDtypeStruct((sum(p.shape[0] for p in pieces), pieces[0].shape[1]), BF16),
        scratch_shapes=[pltpu.SemaphoreType.DMA((len(pieces),))],
        compiler_params=pltpu.CompilerParams(vmem_limit_bytes=MIB),
    )(*pieces)


def masked_store(out, grad, mask, first, block):
    wide = row_mask(mask, out.shape[1], first, block)
    for i in range(mask.shape[0]):
        at = pl.ds(i * block, block)
        out[at, :] = grad[i * block:(i + 1) * block] * wide[i:i + 1]


def grads_kernel(n_pieces, n_terms, block, *refs):
    take = iter(refs)
    flipped = next(take)
    terms = [[next(take) for _ in range(n_pieces)] for _ in range(n_terms)]
    masks = [next(take) for _ in range(n_terms)]
    outs = [next(take) for _ in range(n_terms)]
    (joined,) = take
    step = pl.program_id(0)

    for pieces, mask, out in zip(terms, masks, outs):
        at = 0
        for piece in pieces:
            joined[pl.ds(at, piece.shape[0]), :] = piece[...]
            at += piece.shape[0]
        grad = jnp.dot(flipped[...], joined[...], preferred_element_type=F32)
        masked_store(out, grad, mask[...], step * out.shape[1], block)


def flip_kernel(tokens, out):
    @pl.loop(0, tokens.shape[0] // 128)
    def _(i):
        at = pl.ds(pl.multiple_of(i * 128, 128), 128)
        out[:, at] = tokens[at, :].T


def flip(tokens):
    return pl.pallas_call(
        flip_kernel,
        in_specs=[pl.BlockSpec(memory_space=pltpu.VMEM)],
        out_specs=pl.BlockSpec(memory_space=pltpu.VMEM),
        out_shape=jax.ShapeDtypeStruct(tokens.shape[::-1], tokens.dtype),
        compiler_params=pltpu.CompilerParams(vmem_limit_bytes=6 * MIB),
    )(tokens)


def weight_grads(flipped, terms, masks, wide=WIDE):
    features, total = flipped.shape
    n_terms, n_pieces = len(masks), len(terms[0])
    width = terms[0][0].shape[1]
    steps = width // wide
    whole = pl.BlockSpec(memory_space=pltpu.VMEM)
    block = features // masks[0].shape[0]
    out_spec = pl.BlockSpec((features, wide), lambda f: (0, f))
    return pl.pallas_call(
        functools.partial(grads_kernel, n_pieces, n_terms, block),
        grid=(steps,),
        in_specs=[whole]
        + [pl.BlockSpec((p.shape[0], wide), lambda f: (0, f)) for pieces in terms for p in pieces]
        + [whole] * n_terms,
        out_specs=[out_spec] * n_terms,
        out_shape=[jax.ShapeDtypeStruct((features, width), F32)] * n_terms,
        scratch_shapes=[pltpu.VMEM((total, wide), BF16)],
        compiler_params=pltpu.CompilerParams(vmem_limit_bytes=32 * MIB),
    )(flipped, *[p for pieces in terms for p in pieces], *masks)


def partial(tokens, weight):
    return jnp.dot(tokens, weight, preferred_element_type=F32) * SCALE


def sum_first(tokens, weight):
    from_left = send(partial(tokens[384:640], weight).astype(F16), "first", 1)
    from_right = send(partial(tokens[640:896], weight).astype(F16), "first", -1)
    low = (partial(tokens[256:384], weight) + from_left[128:].astype(F32)).astype(F16)
    low_left = send(low, "first", 1)
    high = (partial(tokens[896:], weight) + from_right[:128].astype(F32)).astype(F16)
    high_right = send(high, "first", -1)
    low = partial(tokens[:128], weight) + from_right[128:].astype(F32) + low_left.astype(F32)
    low = low.astype(F16)
    high = partial(tokens[128:256], weight) + from_left[:128].astype(F32) + high_right.astype(F32)
    high = high.astype(F16)
    return low, high


def sum_second(low, high):
    got = [send(values, "second", shift) for shift, values in ((1, low[64:]), (3, high[64:]), (2, high[:64]))]
    total = low[:64].astype(F32)
    for values in got:
        total = total + values.astype(F32)
    return total * (1.0 / SCALE)


def gather_second(values):
    got = {shift: send(values, "second", -shift) for shift in (1, 3, 2)}
    return [values, got[1], got[2], got[3]]


def gather_first(mine):
    left, right = send(mine, "first", 1), send(mine, "first", -1)
    far_low = send(left[:128], "first", 1)
    far_high = send(right[128:], "first", -1)
    return [mine, right, far_low, far_high, left]


def gather_first_two(one, two):
    one_left, two_right = send(one, "first", 1), send(two, "first", -1)
    two_left, one_right = send(two, "first", 1), send(one, "first", -1)
    one_far, two_far = send(one_left, "first", 1), send(two_right, "first", -1)
    return [one, one_right, one_far, one_left], [two, two_right, two_far, two_left]


def gather_tokens(own, joined):
    mine = {0: own}
    for shift in (1, 3, 2):
        mine[shift] = send(own, "z", -shift)
    pieces = [mine[i] for i in range(SIDE)]
    if joined:
        return place_tokens(pieces + [send(join_rows(pieces), "core", 1)])
    theirs = {shift: send(mine[shift], "core", 1) for shift in (0, 1, 3, 2)}
    return place_tokens(pieces + [theirs[i] for i in range(SIDE)])


def chip_kernel(sizes, *refs):
    count = len(sizes)
    mine, theirs, (own, *outs), (kept, came, sems) = refs[:count], refs[count:2 * count], refs[2 * count:-3], refs[-3:]
    copies = []
    at = 0
    for i, size in enumerate(sizes):
        to = pl.ds(at, size)
        copies.append(pltpu.make_async_copy(mine[i].at[:, 0], kept.at[to], sems.at[0, i]))
        copies.append(pltpu.make_async_copy(theirs[i].at[:, 1], came.at[to], sems.at[1, i]))
        at += size
    for copy in copies:
        copy.start()
    for copy in copies:
        copy.wait()

    @pl.loop(0, SIDE)
    def _(near):
        for far in range(SIDE):
            total = kept[near * SIDE + far] + came[far * SIDE + near]
            at = pl.ds(pl.multiple_of((near * SIDE + far) * 8, 8), 8)
            own[at, :] = total[:8]
            for z, out in enumerate(outs):
                out[at, :] = total[(z + 1) * 8:(z + 2) * 8].astype(BF16)


def chip_sum(mine, theirs):
    features = mine[0].shape[1]
    sizes = tuple(p.shape[0] // 64 for p in mine)
    shape = (sum(p.shape[0] for p in mine) // 8, features)
    whole = pl.BlockSpec(memory_space=pltpu.VMEM)
    return pl.pallas_call(
        functools.partial(chip_kernel, sizes),
        in_specs=[pl.BlockSpec(memory_space=pl.ANY)] * (2 * len(sizes)),
        out_specs=[whole] * SIDE,
        out_shape=[jax.ShapeDtypeStruct(shape, F32)] + [jax.ShapeDtypeStruct(shape, BF16)] * (SIDE - 1),
        scratch_shapes=[pltpu.VMEM((16, 32, features), F32)] * 2 + [pltpu.SemaphoreType.DMA((2, len(sizes)))],
        compiler_params=pltpu.CompilerParams(vmem_limit_bytes=6 * MIB),
        name="chip_sum",
    )(*[p.reshape(-1, 2, 32, features) for p in (*mine, *theirs)])


def back_product(groups):
    mine, theirs = [], []
    for pieces in groups:
        parts = [
            sum(lax.dot_general(t, w, (((1,), (1,)), ((), ())), preferred_element_type=F32) for t, w in pairs)
            for pairs in pieces
        ]
        mine.append(jnp.concatenate(parts, axis=0))
        theirs.append(send(mine[-1], "core", 1))
    own, *parts = chip_sum(mine, theirs)
    got = [send(parts[z - 1], "z", z) for z in (1, 3, 2)]
    return unroll_sum(own, got)


def per_device(
    tokens, out_grad, gate_weight, up_weight, down_weight, gate_mask, up_mask, down_mask
):
    w_gate_up = mask_weights((gate_weight, up_weight), (gate_mask, up_mask), 8)
    w_down = mask_weights((down_weight,), (down_mask,), 8)
    width = w_down.shape[1]

    ins = gather_tokens(tokens, False)
    outs = gather_tokens(out_grad, True)
    near_gate_up = sum_first(ins, w_gate_up)
    near_grad = sum_first(outs, w_down)

    gate_up = sum_second(*near_gate_up)
    gate, up = gate_up[:, :width], gate_up[:, width:]
    hidden = gather_second((gate * jax.nn.sigmoid(gate) * up).astype(BF16))
    hidden = gather_first(jnp.concatenate(hidden, axis=0))

    grad = sum_second(*near_grad)
    gate, up, grad = lax.optimization_barrier((gate, up, grad))
    sig = jax.nn.sigmoid(gate)
    act = gate * sig
    gate_term = (grad * up * sig * (1.0 + gate * (1.0 - sig))).astype(BF16)
    up_term = (grad * act).astype(BF16)
    terms = gather_second(jnp.concatenate([gate_term, up_term], axis=1))
    terms = gather_first_two(
        jnp.concatenate([t[:, :width] for t in terms], axis=0), jnp.concatenate([t[:, width:] for t in terms], axis=0)
    )

    outs_flipped = flip(outs)
    ins_flipped = flip(ins)

    w_pair = w_gate_up[:, :width], w_gate_up[:, width:]
    output = back_product([[[(h, w_down)] for h in hidden]])
    (down_grad,) = weight_grads(outs_flipped, [hidden], [down_mask])
    in_grad = back_product([[list(zip(pair, w_pair))] for pair in zip(*terms)])
    gate_grad, up_grad = weight_grads(ins_flipped, terms, [gate_mask, up_mask])
    return (output, in_grad, gate_grad, up_grad, down_grad)


def solution(mesh):
    data, weight = P(("col", "depth"), "row"), P("row", ("col", "depth"))

    return jax.shard_map(
        per_device,
        mesh=mesh,
        in_specs=(data,) * 2 + (weight,) * 6,
        out_specs=(data,) * 2 + (weight,) * 3,
        check_vma=False,
    )
```

```python
import functools

import jax
import jax.numpy as jnp
from jax import lax
from jax.experimental import pallas as pl
from jax.experimental.pallas import tpu as pltpu
from jax.sharding import PartitionSpec as P


BF16 = jnp.bfloat16
F16 = jnp.float16
F32 = jnp.float32
SIDE = 4
SCALE = 16.0
MIB = 1 << 20
WIDE = 256


def send(values, axis, shift):
    if axis == "core":
        return lax.ppermute(values, "depth", [(0, 1), (1, 0)])
    if axis == "z":
        return lax.ppermute(values, "col", [(z, (z + shift) % SIDE) for z in range(SIDE)])
    perm = []
    for y in range(SIDE):
        for x in range(SIDE):
            for core in range(2):
                along_x = (core == 0) == (axis == "first")
                to_y, to_x = (y, (x + shift) % SIDE) if along_x else ((y + shift) % SIDE, x)
                perm.append(((y * SIDE + x) * 2 + core, (to_y * SIDE + to_x) * 2 + core))
    return lax.ppermute(values, ("row", "depth"), perm)


def row_mask(mask, width, first, block):
    rows = lax.broadcasted_iota(jnp.int32, (mask.shape[1], width), 0)
    cols = lax.broadcasted_iota(jnp.int32, (mask.shape[1], width), 1) + first
    spread = jnp.logical_and(cols >= rows * block, cols < (rows + 1) * block).astype(F32)
    return jnp.dot(mask.astype(F32), spread, preferred_element_type=F32)


def mask_kernel(block, count, *refs):
    masks, weights, out = refs[:count], refs[count:-1], refs[-1]
    width = weights[0].shape[1]
    for j, (mask, weight) in enumerate(zip(masks, weights)):
        wide = row_mask(jnp.broadcast_to(mask[0], (8, mask.shape[2])), width, 0, block)
        out[:, pl.ds(j * width, width)] = (weight[...].astype(F32) * wide[0:1]).astype(BF16)


def mask_weights(weights, masks, vmem):
    rows, width = weights[0].shape
    count, (mrows, mcols) = len(weights), masks[0].shape
    block = rows // mrows
    return pl.pallas_call(
        functools.partial(mask_kernel, block, count),
        grid=(mrows,),
        in_specs=[pl.BlockSpec((1, 1, mcols), lambda i: (i, 0, 0))] * count
        + [pl.BlockSpec((block, width), lambda i: (i, 0))] * count,
        out_specs=pl.BlockSpec((block, count * width), lambda i: (i, 0)),
        out_shape=jax.ShapeDtypeStruct((rows, count * width), BF16),
        compiler_params=pltpu.CompilerParams(vmem_limit_bytes=vmem * MIB),
    )(*[m.reshape(mrows, 1, mcols) for m in masks], *weights)


def spread_mask(weight, mask):
    (rows, width), (mrows, mcols) = weight.shape, mask.shape
    pick = jnp.arange(width) // (width // mcols) == jnp.arange(mcols)[:, None]
    wide = jnp.dot(mask.astype(BF16), pick.astype(BF16), preferred_element_type=F32).astype(BF16)
    return (weight.reshape(mrows, rows // mrows, width) * wide[:, None, :]).reshape(rows, width)


def token_row(near, far):
    row, core = lax.axis_index("row"), lax.axis_index("depth")
    y, x = row // SIDE, lax.rem(row, SIDE)
    to_x = lax.rem(x + jnp.where(core == 0, near, far), SIDE)
    to_y = lax.rem(y + jnp.where(core == 0, far, near), SIDE)
    return pl.multiple_of((to_x * SIDE + to_y) * 8, 8)


def unroll_kernel(own, *refs):
    *got, out = refs
    total = own[...]
    for ref in got:
        total = total + ref[...].astype(F32)
    for i in range(16):
        out[pl.ds(token_row(i // SIDE, i % SIDE), 8), :] = total[i * 8:(i + 1) * 8]


def unroll_sum(own, got):
    whole = pl.BlockSpec(memory_space=pltpu.VMEM)
    return pl.pallas_call(
        unroll_kernel,
        in_specs=[whole] * (1 + len(got)),
        out_specs=whole,
        out_shape=jax.ShapeDtypeStruct(own.shape, F32),
        compiler_params=pltpu.CompilerParams(vmem_limit_bytes=4 * MIB),
        name="unroll_sum",
    )(own, *got)


def place_kernel(*refs):
    *pieces, out = refs
    slots = [(ref, at) for ref in pieces for at in range(0, ref.shape[0], 128)]

    @pl.loop(0, SIDE)
    def _(near):
        for far in range(SIDE):
            start = token_row(near, far)
            for i, (ref, at) in enumerate(slots):
                to = pl.multiple_of((near * SIDE + far) * 64 + i * 8, 8)
                out[pl.ds(to, 8), :] = ref[pl.ds(pl.multiple_of(at + start, 8), 8), :]


def place_tokens(pieces):
    whole = pl.BlockSpec(memory_space=pltpu.VMEM)
    rows = sum(p.shape[0] for p in pieces)
    return pl.pallas_call(
        place_kernel,
        in_specs=[whole] * len(pieces),
        out_specs=whole,
        out_shape=jax.ShapeDtypeStruct((rows, pieces[0].shape[1]), BF16),
        compiler_params=pltpu.CompilerParams(vmem_limit_bytes=6 * MIB),
    )(*pieces)


def join_kernel(*refs):
    *pieces, out, sems = refs
    copies = []
    for i, piece in enumerate(pieces):
        rows = piece.shape[0]
        copies.append(pltpu.make_async_copy(piece, out.at[pl.ds(i * rows, rows), :], sems.at[i]))
    for copy in copies:
        copy.start()
    for copy in copies:
        copy.wait()


def join_rows(pieces):
    return pl.pallas_call(
        join_kernel,
        in_specs=[pl.BlockSpec(memory_space=pl.ANY)] * len(pieces),
        out_specs=pl.BlockSpec(memory_space=pl.ANY),
        out_shape=jax.ShapeDtypeStruct((sum(p.shape[0] for p in pieces), pieces[0].shape[1]), BF16),
        scratch_shapes=[pltpu.SemaphoreType.DMA((len(pieces),))],
        compiler_params=pltpu.CompilerParams(vmem_limit_bytes=MIB),
    )(*pieces)


def masked_store(out, grad, mask, first, block):
    wide = row_mask(mask, out.shape[1], first, block)
    for i in range(mask.shape[0]):
        at = pl.ds(i * block, block)
        out[at, :] = grad[i * block:(i + 1) * block] * wide[i:i + 1]


def grads_kernel(n_pieces, n_terms, block, *refs):
    take = iter(refs)
    flipped = next(take)
    terms = [[next(take) for _ in range(n_pieces)] for _ in range(n_terms)]
    masks = [next(take) for _ in range(n_terms)]
    outs = [next(take) for _ in range(n_terms)]
    (joined,) = take
    step = pl.program_id(0)

    for pieces, mask, out in zip(terms, masks, outs):
        at = 0
        for piece in pieces:
            joined[pl.ds(at, piece.shape[0]), :] = piece[...]
            at += piece.shape[0]
        grad = jnp.dot(flipped[...], joined[...], preferred_element_type=F32)
        masked_store(out, grad, mask[...], step * out.shape[1], block)


def flip_kernel(tokens, out):
    @pl.loop(0, tokens.shape[0] // 128)
    def _(i):
        at = pl.ds(pl.multiple_of(i * 128, 128), 128)
        out[:, at] = tokens[at, :].T


def flip(tokens):
    return pl.pallas_call(
        flip_kernel,
        in_specs=[pl.BlockSpec(memory_space=pltpu.VMEM)],
        out_specs=pl.BlockSpec(memory_space=pltpu.VMEM),
        out_shape=jax.ShapeDtypeStruct(tokens.shape[::-1], tokens.dtype),
        compiler_params=pltpu.CompilerParams(vmem_limit_bytes=6 * MIB),
    )(tokens)


def weight_grads(flipped, terms, masks, wide=WIDE):
    features, total = flipped.shape
    n_terms, n_pieces = len(masks), len(terms[0])
    width = terms[0][0].shape[1]
    steps = width // wide
    whole = pl.BlockSpec(memory_space=pltpu.VMEM)
    block = features // masks[0].shape[0]
    out_spec = pl.BlockSpec((features, wide), lambda f: (0, f))
    return pl.pallas_call(
        functools.partial(grads_kernel, n_pieces, n_terms, block),
        grid=(steps,),
        in_specs=[whole]
        + [pl.BlockSpec((p.shape[0], wide), lambda f: (0, f)) for pieces in terms for p in pieces]
        + [whole] * n_terms,
        out_specs=[out_spec] * n_terms,
        out_shape=[jax.ShapeDtypeStruct((features, width), F32)] * n_terms,
        scratch_shapes=[pltpu.VMEM((total, wide), BF16)],
        compiler_params=pltpu.CompilerParams(vmem_limit_bytes=32 * MIB),
    )(flipped, *[p for pieces in terms for p in pieces], *masks)


def partial(tokens, weight):
    return jnp.dot(tokens, weight, preferred_element_type=F32) * SCALE


def sum_first(tokens, weight):
    from_left = send(partial(tokens[384:640], weight).astype(F16), "first", 1)
    from_right = send(partial(tokens[640:896], weight).astype(F16), "first", -1)
    low = (partial(tokens[256:384], weight) + from_left[128:].astype(F32)).astype(F16)
    low_left = send(low, "first", 1)
    high = (partial(tokens[896:], weight) + from_right[:128].astype(F32)).astype(F16)
    high_right = send(high, "first", -1)
    low = partial(tokens[:128], weight) + from_right[128:].astype(F32) + low_left.astype(F32)
    low = low.astype(F16)
    high = partial(tokens[128:256], weight) + from_left[:128].astype(F32) + high_right.astype(F32)
    high = high.astype(F16)
    return low, high


def sum_second(low, high):
    got = [send(values, "second", shift) for shift, values in ((1, low[64:]), (3, high[64:]), (2, high[:64]))]
    total = low[:64].astype(F32)
    for values in got:
        total = total + values.astype(F32)
    return total * (1.0 / SCALE)


def gather_second(values):
    got = {shift: send(values, "second", -shift) for shift in (1, 3, 2)}
    return [values, got[1], got[2], got[3]]


def gather_first(mine):
    left, right = send(mine, "first", 1), send(mine, "first", -1)
    far_low = send(left[:128], "first", 1)
    far_high = send(right[128:], "first", -1)
    return [mine, right, far_low, far_high, left]


def gather_first_two(one, two):
    one_left, two_right = send(one, "first", 1), send(two, "first", -1)
    two_left, one_right = send(two, "first", 1), send(one, "first", -1)
    one_far, two_far = send(one_left, "first", 1), send(two_right, "first", -1)
    return [one, one_right, one_far, one_left], [two, two_right, two_far, two_left]


def gather_tokens(own, joined):
    mine = {0: own}
    for shift in (1, 3, 2):
        mine[shift] = send(own, "z", -shift)
    pieces = [mine[i] for i in range(SIDE)]
    if joined:
        return place_tokens(pieces + [send(join_rows(pieces), "core", 1)])
    theirs = {shift: send(mine[shift], "core", 1) for shift in (0, 1, 3, 2)}
    return place_tokens(pieces + [theirs[i] for i in range(SIDE)])


def chip_kernel(sizes, *refs):
    count = len(sizes)
    mine, theirs, (own, *outs), (kept, came, sems) = refs[:count], refs[count:2 * count], refs[2 * count:-3], refs[-3:]
    copies = []
    at = 0
    for i, size in enumerate(sizes):
        to = pl.ds(at, size)
        copies.append(pltpu.make_async_copy(mine[i].at[:, 0], kept.at[to], sems.at[0, i]))
        copies.append(pltpu.make_async_copy(theirs[i].at[:, 1], came.at[to], sems.at[1, i]))
        at += size
    for copy in copies:
        copy.start()
    for copy in copies:
        copy.wait()

    @pl.loop(0, SIDE)
    def _(near):
        for far in range(SIDE):
            total = kept[near * SIDE + far] + came[far * SIDE + near]
            at = pl.ds(pl.multiple_of((near * SIDE + far) * 8, 8), 8)
            own[at, :] = total[:8]
            for z, out in enumerate(outs):
                out[at, :] = total[(z + 1) * 8:(z + 2) * 8].astype(BF16)


def chip_sum(mine, theirs):
    features = mine[0].shape[1]
    sizes = tuple(p.shape[0] // 64 for p in mine)
    shape = (sum(p.shape[0] for p in mine) // 8, features)
    whole = pl.BlockSpec(memory_space=pltpu.VMEM)
    return pl.pallas_call(
        functools.partial(chip_kernel, sizes),
        in_specs=[pl.BlockSpec(memory_space=pl.ANY)] * (2 * len(sizes)),
        out_specs=[whole] * SIDE,
        out_shape=[jax.ShapeDtypeStruct(shape, F32)] + [jax.ShapeDtypeStruct(shape, BF16)] * (SIDE - 1),
        scratch_shapes=[pltpu.VMEM((16, 32, features), F32)] * 2 + [pltpu.SemaphoreType.DMA((2, len(sizes)))],
        compiler_params=pltpu.CompilerParams(vmem_limit_bytes=6 * MIB),
        name="chip_sum",
    )(*[p.reshape(-1, 2, 32, features) for p in (*mine, *theirs)])


def back_product(groups):
    mine, theirs = [], []
    for pieces in groups:
        parts = [
            sum(lax.dot_general(t, w, (((1,), (1,)), ((), ())), preferred_element_type=F32) for t, w in pairs)
            for pairs in pieces
        ]
        mine.append(jnp.concatenate(parts, axis=0))
        theirs.append(send(mine[-1], "core", 1))
    own, *parts = chip_sum(mine, theirs)
    got = [send(parts[z - 1], "z", z) for z in (1, 3, 2)]
    return unroll_sum(own, got)


def per_device(
    tokens, out_grad, gate_weight, up_weight, down_weight, gate_mask, up_mask, down_mask
):
    w_gate_up = jnp.concatenate(
        [spread_mask(gate_weight, gate_mask), spread_mask(up_weight, up_mask)], axis=1
    )
    w_down = mask_weights((down_weight,), (down_mask,), 8)
    width = w_down.shape[1]

    ins = gather_tokens(tokens, False)
    outs = gather_tokens(out_grad, True)
    near_gate_up = sum_first(ins, w_gate_up)
    near_grad = sum_first(outs, w_down)

    gate_up = sum_second(*near_gate_up)
    gate, up = gate_up[:, :width], gate_up[:, width:]
    hidden = gather_second((gate * jax.nn.sigmoid(gate) * up).astype(BF16))
    hidden = gather_first(jnp.concatenate(hidden, axis=0))

    grad = sum_second(*near_grad)
    gate, up, grad = lax.optimization_barrier((gate, up, grad))
    sig = jax.nn.sigmoid(gate)
    act = gate * sig
    gate_term = (grad * up * sig * (1.0 + gate * (1.0 - sig))).astype(BF16)
    up_term = (grad * act).astype(BF16)
    terms = gather_second(jnp.concatenate([gate_term, up_term], axis=1))
    terms = gather_first_two(
        jnp.concatenate([t[:, :width] for t in terms], axis=0), jnp.concatenate([t[:, width:] for t in terms], axis=0)
    )

    outs_flipped = flip(outs)
    ins_flipped = flip(ins)

    w_pair = w_gate_up[:, :width], w_gate_up[:, width:]
    output = back_product([[[(h, w_down)] for h in hidden]])
    (down_grad,) = weight_grads(outs_flipped, [hidden], [down_mask], 896)
    in_grad = back_product([[list(zip(pair, w_pair))] for pair in zip(*terms)])
    gate_grad, up_grad = weight_grads(ins_flipped, terms, [gate_mask, up_mask])
    return (output, in_grad, gate_grad, up_grad, down_grad)


def solution(mesh):
    data, weight = P(("col", "depth"), "row"), P("row", ("col", "depth"))

    return jax.shard_map(
        per_device,
        mesh=mesh,
        in_specs=(data,) * 2 + (weight,) * 6,
        out_specs=(data,) * 2 + (weight,) * 3,
        check_vma=False,
    )
```
